128 devices in a mesh: pts: 32 (over z, x, core), grp: 4 (over y).
Axes of the slice: x: 4, y: 4, z: 4, core: 2. Of those that a mesh axis runs over, the one named last changes fastest.
Arguments:
- points: bfloat16 [262144, 256], P(('pts', 'grp')), may hold values from -6 to 6
- rot_dest: int32 [4096], replicated, may hold values from 0 to 4095, as said below
- block_order: int32 [32, 32], P('pts'), may hold values from 0 to 31, each once within a row
- ball_sizes: int32 [32, 8], P('pts'), may hold values from 1 to 8, 32 in all within a row
- fine_gain: float32 [3, 256], replicated, may hold values from 0.1 to 1.9
- fine_qkv: bfloat16 [3, 256, 768], replicated, may hold values from -0.375 to 0.375
- fine_out: bfloat16 [3, 256, 256], replicated, may hold values from -0.375 to 0.375
- pool_weight: bfloat16 [1024, 512], replicated, may hold values from -0.1875 to 0.1875
- coarse_gain: float32 [512], replicated, may hold values from 0.1 to 1.9
- coarse_qkv: bfloat16 [512, 1536], replicated, may hold values from -0.25 to 0.25
- coarse_out: bfloat16 [512, 512], replicated, may hold values from -0.25 to 0.25
- unpool_weight: bfloat16 [512, 1024], replicated, may hold values from -0.25 to 0.25
Outputs:
- refined: bfloat16 [262144, 256], P(('pts', 'grp'))
- coarse: bfloat16 [65536, 512], P(('pts', 'grp'))
The draws below stay inside these ranges and needn't reach their ends.
Inputs may be any that keep to these rules, and one draw needn't show every extreme that they name: A permutation of the sub-blocks. Sub-block s lies on device s // 32 and goes to the device that holds position rot_dest[s]; that device has the same index along grp, and every device sends exactly one sub-block to each device along pts. `block_order`: each row is a permutation. `ball_sizes`: each row sums to 32.
All inputs are finite; a program needn't handle non-finite values.
Results may differ from the reference program's by a relative error of at most 0.012.
Values may be sent and summed in bfloat16 or wider, within the bound.
No kernel may reach another device: no remote copies, remote signals or barrier semaphores. Data moves between devices by JAX's collectives and lax.ppermute only.
A program may use at most 128 MiB of HBM per device.

```python
import math
import jax
import jax.numpy as jnp
import numpy as np
from jax import lax

C = 256
CC = 512
HF = 8
HC = 8
BALL = 256
SUB = 64
CBLK = 64
MOST_BALL = 8
PTS_DEV = 2048
TOKENS = 262144
CB_GROUP = 32
BALLS = 8
N_PTS = 32
N_GRP = 4


def draw_rot_dest(key, part):
    count = PTS_DEV // SUB
    per = count // N_PTS
    first_key, second_key = jax.random.split(jax.random.fold_in(key, 11))
    sources = jax.random.split(first_key, N_GRP * N_PTS)
    targets = jax.random.split(second_key, N_GRP * N_PTS)
    sigma = jax.vmap(lambda k: jax.random.permutation(k, count))(sources).reshape(N_GRP, N_PTS, count).astype(jnp.int32)
    tau = jax.vmap(lambda k: jax.random.permutation(k, count))(targets).reshape(N_GRP, N_PTS, count).astype(jnp.int32)
    target = sigma // per
    index = jnp.arange(N_PTS, dtype=jnp.int32)[None, :, None] * per + sigma % per
    grp_ids = jnp.broadcast_to(jnp.arange(N_GRP, dtype=jnp.int32)[:, None, None], sigma.shape)
    slot = tau[grp_ids, target, index]
    whole = (target * N_GRP + grp_ids) * count + slot
    return jnp.transpose(whole, (1, 0, 2)).reshape(-1).astype(jnp.int32)


def steps_of(stream_key, dims, shards, low, top_value):
    loudness, own = 1.0, jax.random.fold_in(stream_key, 6)
    for position, shards_of in shards:
        steps = jnp.exp(jax.random.uniform(jax.random.fold_in(own, position), (shards_of,), jnp.float32, low / len(shards), top_value / len(shards)))
        loudness = loudness * jnp.repeat(steps, dims[position] // shards_of).reshape([-1 if axis == position else 1 for axis in range(len(dims))])
    return loudness


def split_up(count, total, most, slope):
    weights = [(1 << 20) // math.isqrt(grade ** slope) + 1 for grade in range(2, count + 1)]
    spare, holding = total - most - (count - 1), [1] * (count - 1)
    while spare > 0:
        free = [i for i in range(count - 1) if holding[i] < most]
        whole, remaining = sum([weights[i] for i in free]), spare
        for i in free:
            extra = min(most - holding[i], max(1, remaining * weights[i] // whole), spare)
            holding[i] = holding[i] + extra
            spare = spare - extra
    return np.array([most] + holding)


def ragged(key, amount, total, most, lean):
    if amount == 2:
        one = jax.random.randint(key, (), max(1, total - most), min(most, total - 1) + 1)
        return jnp.stack([one, total - one])
    lengths = jnp.asarray(split_up(amount, total, most, lean), jnp.int32)
    twos = (amount - 1) // 2
    source_of, sink = lengths[1:1 + 2 * twos:2], lengths[2:2 + 2 * twos:2]
    margin = jnp.minimum(source_of - 1, most - sink)
    passed = jax.random.randint(jax.random.fold_in(key, 1), (twos,), 0, 1 << 20) % (margin + 1)
    lengths = lengths.at[1:1 + 2 * twos:2].set(source_of - passed).at[2:2 + 2 * twos:2].set(sink + passed)
    return lengths[jax.random.permutation(jax.random.fold_in(key, 2), amount)]


def gaussian(key, shape, deviation, reach, pieces=(), held_as=jnp.bfloat16):
    loudness = steps_of(key, shape, pieces, -0.22, 0.18) if pieces else 1.0
    entries = jax.random.normal(key, shape, jnp.float32) * deviation * loudness
    return jnp.minimum(jnp.maximum(entries, -reach), reach).astype(held_as)


def setup_inputs(seed: int = 0) -> dict:
    streams_of = jax.random.split(jax.random.key(seed), 13)
    points = gaussian(streams_of[0], (TOKENS, C), 1.0, 6.0, ((0, 128),))
    rot_dest = draw_rot_dest(jax.random.fold_in(streams_of[12], 71), 0)
    block_order = jax.vmap(lambda own: jax.random.permutation(own, CB_GROUP))(jax.random.split(streams_of[2], N_PTS)).reshape((N_PTS, CB_GROUP)).astype(jnp.int32)
    ball_sizes = jax.vmap(lambda own: ragged(own, BALLS, CB_GROUP, MOST_BALL, 2))(jax.random.split(streams_of[3], N_PTS)).reshape((N_PTS, BALLS)).astype(jnp.int32)
    fine_gain = jnp.clip(1.0 + 0.18 * jax.random.normal(streams_of[4], (3, C), jnp.float32), 0.1, 1.9)
    fine_qkv = gaussian(streams_of[5], (3, C, 3 * C), C ** -0.5, 0.375)
    fine_out = gaussian(streams_of[6], (3, C, C), C ** -0.5, 0.375)
    pool_weight = gaussian(streams_of[7], (4 * C, CC), (4 * C) ** -0.5, 0.1875)
    coarse_gain = jnp.clip(1.0 + 0.18 * jax.random.normal(streams_of[8], (CC,), jnp.float32), 0.1, 1.9)
    coarse_qkv = gaussian(streams_of[9], (CC, 3 * CC), CC ** -0.5, 0.25)
    coarse_out = gaussian(streams_of[10], (CC, CC), CC ** -0.5, 0.25)
    unpool_weight = gaussian(streams_of[11], (CC, 4 * C), CC ** -0.5, 0.25)
    return dict(points=points, rot_dest=rot_dest, block_order=block_order, ball_sizes=ball_sizes, fine_gain=fine_gain, fine_qkv=fine_qkv, fine_out=fine_out, pool_weight=pool_weight, coarse_gain=coarse_gain, coarse_qkv=coarse_qkv, coarse_out=coarse_out, unpool_weight=unpool_weight)


def norm_rows(values, gain):
    wide = values.astype(jnp.float32)
    scale = lax.rsqrt(lax.optimization_barrier(jnp.mean(wide * wide, axis=-1, keepdims=True)) + 1e-06)
    return (wide * scale * gain).astype(jnp.bfloat16)

def ball_block(values, gain, w_qkv, w_out):
    rows, width = values.shape
    normed = norm_rows(values, gain)
    packed = jnp.dot(normed, w_qkv, preferred_element_type=jnp.float32).astype(jnp.bfloat16)
    size = width // HF
    balls = rows // BALL
    group = max(1, min(balls, 512 // BALL))
    packed = packed.reshape(balls // group, group, BALL, 3, HF, size)

    def attend(piece):
        query = piece[:, :, 0].astype(jnp.float32)
        keys = piece[:, :, 1].astype(jnp.float32)
        vals = piece[:, :, 2].astype(jnp.float32)
        scores = jnp.einsum('gqhd,gkhd->ghqk', query, keys) / jnp.sqrt(jnp.float32(size))
        top = lax.optimization_barrier(jnp.max(scores, axis=-1, keepdims=True))
        expo = jnp.exp(scores - top)
        probs = (expo / lax.optimization_barrier(jnp.sum(expo, axis=-1, keepdims=True))).astype(jnp.bfloat16)
        out = jnp.einsum('ghqk,gkhd->gqhd', probs.astype(jnp.float32), vals)
        return out.astype(jnp.bfloat16)
    outs = lax.map(attend, packed).reshape(rows, width)
    mixed = jnp.dot(outs, w_out, preferred_element_type=jnp.float32)
    return (values.astype(jnp.float32) + mixed).astype(jnp.bfloat16)

def rotated_layer(values, rot_dest, gain, w_qkv, w_out):
    rows, width = values.shape
    blocks = values.reshape(rows // SUB, SUB, width)
    turned = jnp.zeros_like(blocks).at[rot_dest].set(blocks)
    done = ball_block(turned.reshape(rows, width), gain, w_qkv, w_out)
    return done.reshape(blocks.shape)[rot_dest].reshape(rows, width)

def ball_table(order, sizes):
    count = order.shape[0]
    ends = jnp.cumsum(sizes).astype(jnp.int32)
    starts = (ends - sizes).astype(jnp.int32)
    marks = jnp.arange(count, dtype=jnp.int32)
    where = lax.optimization_barrier(jnp.sum(jnp.where(order[None, :] == marks[:, None], marks[None, :], 0), axis=1)).astype(jnp.int32)
    owner = lax.optimization_barrier(jnp.sum((ends[None, :] <= where[:, None]).astype(jnp.int32), axis=1)).astype(jnp.int32)
    first = starts[owner]
    length = sizes[owner]
    slots = jnp.arange(MOST_BALL, dtype=jnp.int32)
    place = jnp.minimum(first[:, None] + slots[None, :], count - 1).astype(jnp.int32)
    return (order[place], slots[None, :] < length[:, None])

def coarse_attend(query, keys, vals, valid):
    blocks, rows, width = query.shape
    size = width // HC
    query = query.astype(jnp.float32).reshape(blocks, rows, HC, size)
    keys = keys.astype(jnp.float32).reshape(blocks, MOST_BALL * rows, HC, size)
    vals = vals.astype(jnp.float32).reshape(blocks, MOST_BALL * rows, HC, size)
    mask = jnp.broadcast_to(valid[:, :, None], (blocks, MOST_BALL, rows)).reshape(blocks, MOST_BALL * rows)
    scores = jnp.einsum('bqhd,bkhd->bhqk', query, keys) / jnp.sqrt(jnp.float32(size))
    scores = jnp.where(mask[:, None, None, :], scores, -jnp.inf)
    top = lax.optimization_barrier(jnp.max(scores, axis=-1, keepdims=True))
    expo = jnp.exp(scores - top)
    probs = (expo / lax.optimization_barrier(jnp.sum(expo, axis=-1, keepdims=True))).astype(jnp.bfloat16)
    out = jnp.einsum('bhqk,bkhd->bqhd', probs.astype(jnp.float32), vals)
    return out.reshape(blocks, rows, width).astype(jnp.bfloat16)

def reference(points, rot_dest, block_order, ball_sizes, fine_gain, fine_qkv, fine_out, pool_weight, coarse_gain, coarse_qkv, coarse_out, unpool_weight):
    rows, width = points.shape
    first = ball_block(points, fine_gain[0], fine_qkv[0], fine_out[0])
    second = rotated_layer(first, rot_dest, fine_gain[1], fine_qkv[1], fine_out[1])
    pooled = jnp.dot(second.reshape(rows // 4, 4 * width), pool_weight, preferred_element_type=jnp.float32).astype(jnp.bfloat16)
    normed = norm_rows(pooled, coarse_gain)
    cpacked = jnp.dot(normed, coarse_qkv, preferred_element_type=jnp.float32).astype(jnp.bfloat16)
    groups = cpacked.reshape(N_PTS, CB_GROUP, CBLK, 3 * CC)

    def per_group(items):
        packed, order, sizes = items
        members, valid = ball_table(order, sizes)
        query = packed[:, :, :CC]
        keys = packed[:, :, CC:2 * CC][members]
        vals = packed[:, :, 2 * CC:][members]
        return coarse_attend(query, keys, vals, valid)
    cattended = lax.map(per_group, (groups, block_order, ball_sizes)).reshape(rows // 4, CC)
    coarse = (pooled.astype(jnp.float32) + jnp.dot(cattended, coarse_out, preferred_element_type=jnp.float32)).astype(jnp.bfloat16)
    lifted = jnp.dot(coarse, unpool_weight, preferred_element_type=jnp.float32).reshape(rows, width)
    third = (second.astype(jnp.float32) + lifted).astype(jnp.bfloat16)
    refined = rotated_layer(third, rot_dest, fine_gain[2], fine_qkv[2], fine_out[2])
    return (refined, coarse)
```

```python
import functools
import math

import jax
import jax.numpy as jnp
from jax import lax
from jax.experimental import pallas as pl
from jax.experimental.pallas import tpu as pltpu
from jax.sharding import PartitionSpec as P

F32, BF16 = jnp.float32, jnp.bfloat16
HEADS = 8
BALL = 256
SUB = 64
CBLK = 64
MOST_BALL = 8
WIDTH = 256
CWIDTH = 512
SUBS = 32
POOL = 16
LOG2E = 1.4426950408889634
NT = (((1,), (1,)), ((), ()))
TN = (((0,), (0,)), ((), ()))
VMEM = pl.BlockSpec(memory_space=pltpu.VMEM)
SMEM = pl.BlockSpec(memory_space=pltpu.SMEM)


def dot(a, b, dims=None):
    if dims is None:
        return jnp.dot(a, b, preferred_element_type=F32)
    return lax.dot_general(a, b, dims, preferred_element_type=F32)


def norm(x, gain):
    return (x * lax.rsqrt(jnp.mean(x * x, axis=-1, keepdims=True) + 1e-6) * gain).astype(BF16)


def head_masks():
    lane = lax.broadcasted_iota(jnp.int32, (1, 128), 1) // 32
    return [(lane == i).astype(F32).astype(BF16) for i in range(4)]


def fine_mixed(h, wqkv, wvt, wo, masks):
    q = (dot(h, wqkv[:, :WIDTH]) * (LOG2E / math.sqrt(32.0))).astype(BF16)
    k = dot(h, wqkv[:, WIDTH : 2 * WIDTH]).astype(BF16)
    vt = dot(wvt, h, NT).astype(BF16)
    ones = jnp.ones((16, BALL), BF16)
    heads = []
    for g in range(2):
        kg = k[:, 128 * g : 128 * g + 128]
        qg = q[:, 128 * g : 128 * g + 128]
        kc = jnp.concatenate([kg * masks[i] for i in range(4)], axis=0)
        sc = dot(kc, qg, NT)
        for i in range(4):
            head = 4 * g + i
            s = sc[BALL * i : BALL * (i + 1)]
            top = jnp.max(s, axis=0, keepdims=True)
            p = jnp.exp2(s - top).astype(BF16)
            o = dot(jnp.concatenate([vt[32 * head : 32 * head + 32], ones], axis=0), p)
            heads.append((o[:32] * (1.0 / o[32:33])).astype(BF16))
    return dot(jnp.concatenate(heads, axis=0), wo, TN)


def gathered(ref, table, b):
    return jnp.concatenate([ref[table[4 * b + i]] for i in range(4)], axis=0)


def first_kernel(tables, x_ref, gain_ref, wqkv_ref, wo_ref, out_ref, wvt_ref):
    wvt_ref[...] = wqkv_ref[:, 2 * WIDTH :].T
    masks = head_masks()

    def ball(b, carry):
        x = x_ref[pl.ds(4 * b, 4)].reshape(BALL, WIDTH).astype(F32)
        h = norm(x, gain_ref[...])
        y = (x + fine_mixed(h, wqkv_ref[...], wvt_ref[...], wo_ref[...], masks)).astype(BF16)
        for i in range(4):
            out_ref[tables[0, 4 * b + i]] = y[SUB * i : SUB * (i + 1)]
        return carry

    lax.fori_loop(0, SUBS // 4, ball, 0)


def second_kernel(
    tables, x_ref, gain_ref, wqkv_ref, wo_ref, pool_ref, out_ref, pooled_ref, wvt_ref, wide_ref
):
    wvt_ref[...] = wqkv_ref[:, 2 * WIDTH :].T
    masks = head_masks()

    def ball(b, carry):
        x = jnp.concatenate([x_ref[tables[1, 4 * b + i]] for i in range(4)], axis=0).astype(F32)
        h = norm(x, gain_ref[...])
        y = (x + fine_mixed(h, wqkv_ref[...], wvt_ref[...], wo_ref[...], masks)).astype(BF16)
        out_ref[b] = y
        wide = y.astype(F32)
        for c in range(2):
            wide_ref[c] = wide[:, 128 * c : 128 * c + 128]
        rows = jnp.concatenate(
            [wide_ref[c, pl.ds(j, BALL // 4, stride=4)] for j in range(4) for c in range(2)],
            axis=1,
        ).astype(BF16)
        pooled = dot(rows, pool_ref[...]).astype(BF16)
        for i in range(4):
            pooled_ref[tables[1, 4 * b + i]] = pooled[POOL * i : POOL * (i + 1)]
        return carry

    lax.fori_loop(0, SUBS // 4, ball, 0)


def third_kernel(
    tables, x_ref, coarse_ref, gain_ref, wqkv_ref, wo_ref, unpool_ref, out_ref, wvt_ref, wide_ref
):
    wvt_ref[...] = wqkv_ref[:, 2 * WIDTH :].T
    masks = head_masks()

    def ball(b, carry):
        coarse = jnp.concatenate([coarse_ref[tables[1, 4 * b + i]] for i in range(4)], axis=0)
        lifted = dot(coarse, unpool_ref[...])
        for j in range(4):
            for c in range(2):
                at = WIDTH * j + 128 * c
                wide_ref[c, pl.ds(j, BALL // 4, stride=4)] = lifted[:, at : at + 128]
        x = x_ref[b].astype(F32) + jnp.concatenate([wide_ref[0], wide_ref[1]], axis=1)
        x = x.astype(BF16).astype(F32)
        h = norm(x, gain_ref[...])
        y = (x + fine_mixed(h, wqkv_ref[...], wvt_ref[...], wo_ref[...], masks)).astype(BF16)
        for i in range(4):
            out_ref[tables[1, 4 * b + i]] = y[SUB * i : SUB * (i + 1)]
        return carry

    lax.fori_loop(0, SUBS // 4, ball, 0)


def ordered_kernel(tables, x_ref, out_ref):
    for s in range(SUBS):
        out_ref[s] = x_ref[tables[0, s]]


def coarse_start_kernel(tables, pieces_ref, gain_ref, pooled_ref, normed_ref):
    for s in range(SUBS):
        piece = pieces_ref[tables[0, s]]
        pooled_ref[POOL * s : POOL * (s + 1)] = piece
    normed_ref[...] = norm(pooled_ref[...].astype(F32), gain_ref[...])


def project_kernel(*refs):
    count = (len(refs) - 1) // 2
    w_ref = refs[count]
    for x_ref, out_ref in zip(refs[:count], refs[count + 1 :]):
        out_ref[...] = dot(x_ref[...], w_ref[...]).astype(BF16)


def coarse_kernel(
    tables,
    blocks,
    counts,
    pooled_ref,
    own_ref,
    left_ref,
    right_ref,
    far_a_ref,
    far_b_ref,
    wkv_ref,
    wo_ref,
    coarse_ref,
    sent_ref,
    kv_ref,
    att_ref,
    *,
    groups,
):
    me = tables[2, 0]
    rows = CWIDTH
    for step, ref in ((0, own_ref), (groups - 1, left_ref), (1, right_ref)):
        at = pl.multiple_of(lax.rem(me + step, groups) * rows, rows)
        kv_ref[pl.ds(at, rows)] = ref[:, ref.shape[1] - 2 * CWIDTH :]
    at = pl.multiple_of(lax.rem(me + 2, groups) * rows, rows)
    half = rows // 2
    kv_ref[pl.ds(at, half)] = dot(far_a_ref[...], wkv_ref[...]).astype(BF16)
    kv_ref[pl.ds(at + half, half)] = dot(far_b_ref[...], wkv_ref[...]).astype(BF16)
    size = 64
    lanes = lax.broadcasted_iota(jnp.int32, (1, 256), 1) // size
    keep = [(lanes == i).astype(F32) for i in range(4)]
    keep_low = [m.astype(BF16) for m in keep]
    member = lax.broadcasted_iota(jnp.int32, (1, MOST_BALL * CBLK), 1) // CBLK

    def block(b, carry):
        valid = member < counts[b]
        starts = [pl.multiple_of(blocks[b * MOST_BALL + m] * CBLK, CBLK) for m in range(MOST_BALL)]
        begin = pl.multiple_of(b * CBLK, CBLK)
        for g in range(2):
            q = own_ref[pl.ds(begin, CBLK), 256 * g : 256 * g + 256]
            spread = jnp.concatenate([q * keep_low[i] for i in range(4)], axis=0)
            keys = jnp.concatenate(
                [kv_ref[pl.ds(s, CBLK), 256 * g : 256 * g + 256] for s in starts], axis=0
            )
            vals = jnp.concatenate(
                [kv_ref[pl.ds(s, CBLK), CWIDTH + 256 * g : CWIDTH + 256 * g + 256] for s in starts],
                axis=0,
            )
            scores = jnp.where(valid, dot(spread, keys, NT) * (LOG2E / 8.0), -jnp.inf)
            top = jnp.max(scores, axis=-1, keepdims=True)
            expo = jnp.exp2(scores - top)
            probs = (expo * (1.0 / jnp.sum(expo, axis=-1, keepdims=True))).astype(BF16)
            out = dot(probs, vals)
            total = sum(out[CBLK * i : CBLK * (i + 1)] * keep[i] for i in range(4))
            att_ref[pl.ds(begin, CBLK), 256 * g : 256 * g + 256] = total.astype(BF16)
        return carry

    lax.fori_loop(0, rows // CBLK, block, 0)
    result = (pooled_ref[...].astype(F32) + dot(att_ref[...], wo_ref[...])).astype(BF16)
    coarse_ref[...] = result
    for s in range(SUBS):
        sent_ref[tables[0, s]] = result[POOL * s : POOL * (s + 1)]


def call(kernel, outs, scratch, args, tables=1, flops=0, exps=0, name=None):
    size = sum(a.size * a.dtype.itemsize for a in args)
    return pl.pallas_call(
        kernel,
        out_shape=outs,
        in_specs=[SMEM] * tables + [VMEM] * (len(args) - tables),
        out_specs=jax.tree.map(lambda _: VMEM, outs),
        scratch_shapes=scratch,
        name=name,
        cost_estimate=pl.CostEstimate(flops=flops, bytes_accessed=2 * size, transcendentals=exps),
    )(*args)


def shaped(*shape):
    return jax.ShapeDtypeStruct(shape, BF16)


def exchange(pieces):
    return lax.all_to_all(pieces, "pts", split_axis=0, concat_axis=0, tiled=True)


def tables_of(rot_dest):
    points, groups = lax.axis_size("pts"), lax.axis_size("grp")
    group = lax.axis_index("grp")
    device = lax.axis_index("pts") * groups + group
    target = lax.dynamic_slice_in_dim(rot_dest, device * SUBS, SUBS) // SUBS // groups
    mine = lax.dynamic_index_in_dim(rot_dest.reshape(points, groups, SUBS), group, 1, False)
    slot = mine - device * SUBS
    source = jnp.arange(points, dtype=jnp.int32)
    hit = slot[None] == jnp.arange(SUBS, dtype=jnp.int32)[:, None, None]
    place = jnp.sum(jnp.where(hit, source[None, :, None], 0), axis=(1, 2))
    return jnp.stack([target, place, jnp.broadcast_to(group, (SUBS,))]).astype(jnp.int32)


def ball_table(order, sizes, count):
    total = order.shape[0]
    before = jnp.arange(sizes.shape[0])
    ends = jnp.sum(jnp.where(before[None, :] <= before[:, None], sizes[None, :], 0), axis=1)
    starts = ends - sizes
    marks = jnp.arange(total, dtype=jnp.int32)
    mine = lax.axis_index("grp") * count + jnp.arange(count, dtype=jnp.int32)
    where = jnp.sum(jnp.where(order[None, :] == mine[:, None], marks[None, :], 0), axis=1)
    inside = (starts[None, :] <= where[:, None]) & (where[:, None] < ends[None, :])
    first = jnp.sum(jnp.where(inside, starts[None, :], 0), axis=1)
    length = jnp.sum(jnp.where(inside, sizes[None, :], 0), axis=1)
    slots = jnp.arange(MOST_BALL, dtype=jnp.int32)
    place = jnp.minimum(first[:, None] + slots[None, :], total - 1)
    members = jnp.sum(
        jnp.where(place[:, :, None] == marks[None, None, :], order[None, None, :], 0), axis=2
    )
    return members.reshape(-1).astype(jnp.int32), length.astype(jnp.int32)


def body(
    points,
    rot_dest,
    block_order,
    ball_sizes,
    fine_gain,
    fine_qkv,
    fine_out,
    pool_weight,
    coarse_gain,
    coarse_qkv,
    coarse_out,
    unpool_weight,
):
    rows, width = points.shape
    groups = lax.axis_size("grp")
    crows = rows // 4
    tables = tables_of(rot_dest)
    members, lengths = ball_table(block_order[0], ball_sizes[0], crows // CBLK)
    gains = [fine_gain[j : j + 1] for j in range(3)]
    turn = pltpu.VMEM((width, width), BF16)
    wide = pltpu.VMEM((2, BALL, 128), F32)
    cost = dict(flops=5 * 10**9, exps=4 * 10**6)

    sent = call(
        first_kernel,
        shaped(SUBS, SUB, width),
        [turn],
        (tables, points.reshape(SUBS, SUB, width), gains[0], fine_qkv[0], fine_out[0]),
        name="first_layer",
        **cost,
    )
    arrived = exchange(sent)
    second, pieces = call(
        second_kernel,
        (shaped(SUBS // 4, BALL, width), shaped(SUBS, POOL, CWIDTH)),
        [turn, wide],
        (tables, arrived, gains[1], fine_qkv[1], fine_out[1], pool_weight),
        name="second_layer",
        **cost,
    )
    pieces = exchange(pieces)
    pooled, normed = call(
        coarse_start_kernel,
        (shaped(crows, CWIDTH), shaped(crows, CWIDTH)),
        [],
        (tables, pieces, coarse_gain[None]),
        name="coarse_start",
    )
    up = [(i, (i + 1) % groups) for i in range(groups)]
    down = [(i, (i - 1) % groups) for i in range(groups)]
    half = crows // 2
    left = lax.ppermute(normed, "grp", up)
    right = lax.ppermute(normed, "grp", down)
    own = call(
        project_kernel,
        shaped(crows, 3 * CWIDTH),
        [],
        (normed, coarse_qkv),
        tables=0,
        flops=2 * crows * CWIDTH * 3 * CWIDTH,
        name="own_projection",
    )
    far_a = lax.ppermute(left[:half], "grp", up)
    far_b = lax.ppermute(right[half:], "grp", down)
    wkv = coarse_qkv[:, CWIDTH:]
    left, right = call(
        project_kernel,
        (shaped(crows, 2 * CWIDTH), shaped(crows, 2 * CWIDTH)),
        [],
        (left, right, wkv),
        tables=0,
        flops=8 * crows * CWIDTH * CWIDTH,
        name="near_projection",
    )
    coarse, pieces = call(
        functools.partial(coarse_kernel, groups=groups),
        (shaped(crows, CWIDTH), shaped(SUBS, POOL, CWIDTH)),
        [pltpu.VMEM((groups * crows, 2 * CWIDTH), BF16), pltpu.VMEM((crows, CWIDTH), BF16)],
        (tables, members, lengths, pooled, own, left, right, far_a, far_b, wkv, coarse_out),
        tables=3,
        flops=4 * 10**9,
        exps=2 * 10**6,
        name="coarse_layer",
    )
    pieces = exchange(pieces)
    sent = call(
        third_kernel,
        shaped(SUBS, SUB, width),
        [turn, wide],
        (tables, second, pieces, gains[2], fine_qkv[2], fine_out[2], unpool_weight),
        name="third_layer",
        **cost,
    )
    refined = call(
        ordered_kernel,
        shaped(SUBS, SUB, width),
        [],
        (tables, exchange(sent)),
        name="ordered",
    )
    return refined.reshape(rows, width), coarse


def solution(mesh):
    return jax.shard_map(
        body,
        mesh=mesh,
        in_specs=(
            P(("pts", "grp"), None),
            P(),
            P("pts", None),
            P("pts", None),
            P(),
            P(),
            P(),
            P(),
            P(),
            P(),
            P(),
            P(),
        ),
        out_specs=(P(("pts", "grp"), None), P(("pts", "grp"), None)),
        check_vma=False,
    )
```

```python
import functools
import math

import jax
import jax.numpy as jnp
from jax import lax
from jax.experimental import pallas as pl
from jax.experimental.pallas import tpu as pltpu
from jax.sharding import PartitionSpec as P

F32, BF16 = jnp.float32, jnp.bfloat16
HEADS = 8
BALL = 256
SUB = 64
CBLK = 64
MOST_BALL = 8
WIDTH = 256
CWIDTH = 512
SUBS = 32
POOL = 16
LOG2E = 1.4426950408889634
NT = (((1,), (1,)), ((), ()))
TN = (((0,), (0,)), ((), ()))
VMEM = pl.BlockSpec(memory_space=pltpu.VMEM)
SMEM = pl.BlockSpec(memory_space=pltpu.SMEM)


def dot(a, b, dims=None):
    if dims is None:
        return jnp.dot(a, b, preferred_element_type=F32)
    return lax.dot_general(a, b, dims, preferred_element_type=F32)


def norm(x, gain):
    return (x * lax.rsqrt(jnp.mean(x * x, axis=-1, keepdims=True) + 1e-6) * gain).astype(BF16)


def head_masks():
    lane = lax.broadcasted_iota(jnp.int32, (1, 128), 1) // 32
    return [(lane == i).astype(F32).astype(BF16) for i in range(4)]


SCALE = LOG2E / math.sqrt(32.0)
BALLS = SUBS // 4
VM = pltpu.VMEM


def transposed(wqkv_ref, wqvt_ref):
    wqvt_ref[:WIDTH] = wqkv_ref[:, :WIDTH].T
    wqvt_ref[WIDTH:] = wqkv_ref[:, 2 * WIDTH :].T


def fine_layer(load, reload, store, gain, wqvt_ref, wk_ref, wo_ref, scores, bufs, ready=None):
    left, right = scores
    k_s, qt_s, vt_s, ot_s = bufs[0:2], bufs[2:4], bufs[4:6], bufs[6:8]
    masks = head_masks()
    ones = jnp.ones((16, BALL), BF16)

    def project(b, par):
        h = norm(load(b), gain)
        qv = dot(wqvt_ref[...], h, NT)
        qt_s[par][...] = (qv[:WIDTH] * SCALE).astype(BF16)
        vt_s[par][...] = qv[WIDTH:].astype(BF16)
        k_s[par][...] = dot(h, wk_ref[...]).astype(BF16)

    def score(dst, par, g, i):
        keys = k_s[par][:, 128 * g : 128 * g + 128] * masks[i]
        dst[BALL * i : BALL * (i + 1)] = dot(keys, qt_s[par][128 * g : 128 * g + 128, :])

    def soft(src, par, g, i):
        s = src[BALL * i : BALL * (i + 1)]
        p = jnp.exp2(s - jnp.max(s, axis=0, keepdims=True)).astype(BF16)
        at = 32 * (4 * g + i)
        o = dot(jnp.concatenate([vt_s[par][at : at + 32], ones], axis=0), p)
        ot_s[par][at : at + 32] = (o[:32] * (1.0 / o[32:33])).astype(BF16)

    def finish(b, par):
        store(b, (reload(b) + dot(ot_s[par][...], wo_ref[...], TN)).astype(BF16))

    ot_s[1][...] = jnp.zeros_like(ot_s[1])
    project(0, 0)
    for i in range(4):
        score(left, 0, 0, i)
    if ready is not None:
        ready()

    def step(b, par):
        project(jnp.minimum(b + 1, BALLS - 1), 1 - par)
        for i in range(4):
            score(right, par, 1, i)
            soft(left, par, 0, i)
        finish(jnp.maximum(b - 1, 0), 1 - par)
        for i in range(4):
            score(left, 1 - par, 0, i)
            soft(right, par, 1, i)

    def pair(t, carry):
        step(2 * t, 0)
        step(2 * t + 1, 1)
        return carry

    lax.fori_loop(0, BALLS // 2, pair, 0)
    finish(BALLS - 1, 1)


FINE_SCRATCH = [VM((4 * BALL, BALL), F32)] * 2 + [VM((BALL, WIDTH), BF16)] * 8


def first_kernel(
    rot, gain_ref, x_hbm, wqkv_hbm, wo_hbm, out_ref, wqvt_ref, x_ref, wqkv_ref, wo_ref, sems, *scratch
):
    groups = lax.axis_size("grp")
    device = lax.axis_index("pts") * groups + lax.axis_index("grp")
    copies = [
        pltpu.make_async_copy(wqkv_hbm.at[0], wqkv_ref, sems.at[0]),
        pltpu.make_async_copy(x_hbm.at[pl.ds(0, 4)], x_ref.at[pl.ds(0, 4)], sems.at[1]),
        pltpu.make_async_copy(wo_hbm.at[0], wo_ref, sems.at[2]),
        pltpu.make_async_copy(x_hbm.at[pl.ds(4, SUBS - 4)], x_ref.at[pl.ds(4, SUBS - 4)], sems.at[3]),
    ]
    for copy in copies:
        copy.start()
    copies[0].wait()
    transposed(wqkv_ref, wqvt_ref)
    copies[1].wait()

    def ready():
        copies[2].wait()
        copies[3].wait()

    def load(b):
        return x_ref[pl.ds(4 * b, 4)].reshape(BALL, WIDTH).astype(F32)

    def store(b, y):
        for i in range(4):
            out_ref[rot[device * SUBS + 4 * b + i] // (SUBS * groups)] = y[SUB * i : SUB * (i + 1)]

    wk_ref = wqkv_ref.at[:, WIDTH : 2 * WIDTH]
    fine_layer(
        load, load, store, gain_ref[...], wqvt_ref, wk_ref, wo_ref, scratch[:2], scratch[2:], ready
    )


def second_kernel(
    place, x_ref, gain_ref, wqvt_ref, wk_ref, wo_ref, pool_ref, out_ref, pooled_ref, wide_ref, *scratch
):
    def load(b):
        return jnp.concatenate([x_ref[place[4 * b + i]] for i in range(4)], axis=0).astype(F32)

    def store(b, y):
        out_ref[b] = y
        wide = y.astype(F32)
        for c in range(2):
            wide_ref[c] = wide[:, 128 * c : 128 * c + 128]
        rows = jnp.concatenate(
            [wide_ref[c, pl.ds(j, BALL // 4, stride=4)] for j in range(4) for c in range(2)],
            axis=1,
        ).astype(BF16)
        pooled = dot(rows, pool_ref[...]).astype(BF16)
        for i in range(4):
            pooled_ref[place[4 * b + i]] = pooled[POOL * i : POOL * (i + 1)]

    fine_layer(load, load, store, gain_ref[...], wqvt_ref, wk_ref, wo_ref, scratch[:2], scratch[2:])


def third_kernel(
    place, x_ref, coarse_ref, gain_ref, wqvt_ref, wk_ref, wo_ref, unpool_ref, out_ref,
    wide_ref, held_ref, *scratch
):
    def load(b):
        coarse = jnp.concatenate([coarse_ref[place[4 * b + i]] for i in range(4)], axis=0)
        lifted = dot(coarse, unpool_ref[...])
        for j in range(4):
            for c in range(2):
                at = WIDTH * j + 128 * c
                wide_ref[c, pl.ds(j, BALL // 4, stride=4)] = lifted[:, at : at + 128]
        x = x_ref[b].astype(F32) + jnp.concatenate([wide_ref[0], wide_ref[1]], axis=1)
        held_ref[b] = x.astype(BF16)
        return x.astype(BF16).astype(F32)

    def reload(b):
        return held_ref[b].astype(F32)

    def store(b, y):
        for i in range(4):
            out_ref[place[4 * b + i]] = y[SUB * i : SUB * (i + 1)]

    fine_layer(load, reload, store, gain_ref[...], wqvt_ref, wk_ref, wo_ref, scratch[:2], scratch[2:])


def group_of(step):
    return lax.rem(lax.axis_index("grp") + step, lax.axis_size("grp"))


def tree_rows(pieces, table, group):
    return jnp.concatenate([pieces(table[group, s]) for s in range(SUBS)], axis=0)


def own_kernel(table, pieces_ref, gain_ref, w_ref, pooled_ref, out_ref):
    pooled_ref[...] = tree_rows(lambda k: pieces_ref[k], table, group_of(0))
    out_ref[...] = dot(norm(pooled_ref[...].astype(F32), gain_ref[...]), w_ref[...]).astype(BF16)


def near_kernel(table, la_ref, lb_ref, ra_ref, rb_ref, gain_ref, w_ref, left_ref, right_ref, all_ref):
    groups = lax.axis_size("grp")
    half = SUBS // 2
    for step, a_ref, b_ref, out_ref in ((groups - 1, la_ref, lb_ref, left_ref), (1, ra_ref, rb_ref, right_ref)):
        all_ref[:half] = a_ref[...]
        all_ref[half:] = b_ref[...]
        rows = tree_rows(lambda k: all_ref[k], table, group_of(step)).astype(F32)
        out_ref[...] = dot(norm(rows, gain_ref[...]), w_ref[:, CWIDTH:]).astype(BF16)


def coarse_kernel(
    table, blocks, counts, pooled_ref, own_ref, left_ref, right_ref, far_a_ref, far_b_ref,
    gain_ref, w_ref, wo_ref, coarse_ref, sent_ref, kv_ref, all_ref, att_ref, a_ref, b_ref,
):
    groups = lax.axis_size("grp")
    me = lax.axis_index("grp")
    rows = CWIDTH
    half = SUBS // 2
    all_ref[:half] = far_a_ref[...]
    all_ref[half:] = far_b_ref[...]
    far = norm(tree_rows(lambda k: all_ref[k], table, group_of(2)).astype(F32), gain_ref[...])
    at = pl.multiple_of(group_of(2) * rows, rows)
    kv_ref[pl.ds(at, rows)] = dot(far, w_ref[:, CWIDTH:]).astype(BF16)
    for step, ref in ((0, own_ref), (groups - 1, left_ref), (1, right_ref)):
        at = pl.multiple_of(group_of(step) * rows, rows)
        kv_ref[pl.ds(at, rows)] = ref[:, ref.shape[1] - 2 * CWIDTH :]
    size = 64
    lanes = lax.broadcasted_iota(jnp.int32, (1, 256), 1) // size
    keep = [(lanes == i).astype(F32) for i in range(4)]
    keep_low = [m.astype(BF16) for m in keep]
    member = lax.broadcasted_iota(jnp.int32, (1, MOST_BALL * CBLK), 1) // CBLK

    def members(b, at):
        starts = [pl.multiple_of(blocks[b * MOST_BALL + m] * CBLK, CBLK) for m in range(MOST_BALL)]
        return jnp.concatenate([kv_ref[pl.ds(s, CBLK), at : at + 256] for s in starts], axis=0)

    def score(dst, b, g):
        q = own_ref[pl.ds(pl.multiple_of(b * CBLK, CBLK), CBLK), 256 * g : 256 * g + 256]
        spread = jnp.concatenate([q * keep_low[i] for i in range(4)], axis=0)
        scores = dot(spread, members(b, 256 * g), NT) * (LOG2E / 8.0)
        dst[...] = jnp.where(member < counts[b], scores, -jnp.inf)

    def soft(src, b, g):
        scores = src[...]
        expo = jnp.exp2(scores - jnp.max(scores, axis=-1, keepdims=True))
        scale = 1.0 / jnp.sum(expo, axis=-1, keepdims=True)
        out = dot(expo.astype(BF16), members(b, CWIDTH + 256 * g)) * scale
        total = sum(out[CBLK * i : CBLK * (i + 1)] * keep[i] for i in range(4))
        begin = pl.multiple_of(b * CBLK, CBLK)
        att_ref[pl.ds(begin, CBLK), 256 * g : 256 * g + 256] = total.astype(BF16)

    count = rows // CBLK
    score(a_ref, 0, 0)

    def block(b, carry):
        score(b_ref, b, 1)
        soft(a_ref, b, 0)
        score(a_ref, jnp.minimum(b + 1, count - 1), 0)
        soft(b_ref, b, 1)
        return carry

    lax.fori_loop(0, count, block, 0)
    result = (pooled_ref[...].astype(F32) + dot(att_ref[...], wo_ref[...])).astype(BF16)
    coarse_ref[...] = result
    for s in range(SUBS):
        sent_ref[table[me, s]] = result[POOL * s : POOL * (s + 1)]


def call(kernel, outs, scratch, args, tables=1, flops=0, exps=0, name=None, grant=16, specs=None):
    size = sum(a.size * a.dtype.itemsize for a in args)
    return pl.pallas_call(
        kernel,
        out_shape=outs,
        in_specs=specs or [SMEM] * tables + [VMEM] * (len(args) - tables),
        out_specs=jax.tree.map(lambda _: VMEM, outs),
        scratch_shapes=scratch,
        name=name,
        compiler_params=pltpu.CompilerParams(vmem_limit_bytes=grant << 20),
        cost_estimate=pl.CostEstimate(flops=flops, bytes_accessed=2 * size, transcendentals=exps),
    )(*args)


def shaped(*shape):
    return jax.ShapeDtypeStruct(shape, BF16)


def exchange(pieces):
    return lax.all_to_all(pieces, "pts", split_axis=0, concat_axis=0, tiled=True)


def tables_of(rot_dest):
    points, groups = lax.axis_size("pts"), lax.axis_size("grp")
    point, group = lax.axis_index("pts"), lax.axis_index("grp")
    device = point * groups + group
    local = lax.dynamic_slice_in_dim(rot_dest, point * groups * SUBS, groups * SUBS)
    targets = (local // SUBS // groups).reshape(groups, SUBS)
    mine = lax.dynamic_index_in_dim(rot_dest.reshape(points, groups, SUBS), group, 1, False)
    slot = mine - device * SUBS
    source = jnp.arange(points, dtype=jnp.int32)
    hit = slot[None] == jnp.arange(SUBS, dtype=jnp.int32)[:, None, None]
    place = jnp.sum(jnp.where(hit, source[None, :, None], 0), axis=(1, 2))
    return targets, place.astype(jnp.int32)


def ball_table(order, sizes, count):
    total = order.shape[0]
    before = jnp.arange(sizes.shape[0])
    ends = jnp.sum(jnp.where(before[None, :] <= before[:, None], sizes[None, :], 0), axis=1)
    starts = ends - sizes
    marks = jnp.arange(total, dtype=jnp.int32)
    mine = lax.axis_index("grp") * count + jnp.arange(count, dtype=jnp.int32)
    where = jnp.sum(jnp.where(order[None, :] == mine[:, None], marks[None, :], 0), axis=1)
    inside = (starts[None, :] <= where[:, None]) & (where[:, None] < ends[None, :])
    first = jnp.sum(jnp.where(inside, starts[None, :], 0), axis=1)
    length = jnp.sum(jnp.where(inside, sizes[None, :], 0), axis=1)
    slots = jnp.arange(MOST_BALL, dtype=jnp.int32)
    place = jnp.minimum(first[:, None] + slots[None, :], total - 1)
    members = jnp.sum(
        jnp.where(place[:, :, None] == marks[None, None, :], order[None, None, :], 0), axis=2
    )
    return members.reshape(-1).astype(jnp.int32), length.astype(jnp.int32)


def body(
    points,
    rot_dest,
    block_order,
    ball_sizes,
    fine_gain,
    fine_qkv,
    fine_out,
    pool_weight,
    coarse_gain,
    coarse_qkv,
    coarse_out,
    unpool_weight,
):
    rows, width = points.shape
    groups = lax.axis_size("grp")
    crows = rows // 4
    wide = VM((2, BALL, 128), F32)
    cost = dict(flops=5 * 10**9, exps=4 * 10**6)
    sent = call(
        first_kernel,
        shaped(SUBS, SUB, width),
        [
            VM((2 * width, width), BF16),
            VM((SUBS, SUB, width), BF16),
            VM((width, 3 * width), BF16),
            VM((width, width), BF16),
            pltpu.SemaphoreType.DMA((4,)),
        ]
        + FINE_SCRATCH,
        (rot_dest, fine_gain[0:1], points.reshape(SUBS, SUB, width), fine_qkv, fine_out),
        specs=[SMEM, VMEM] + [pl.BlockSpec(memory_space=pl.ANY)] * 3,
        grant=60,
        name="first_layer",
        **cost,
    )
    sent, rot_dest, block_order, ball_sizes, fine_qkv, fine_out, fine_gain = lax.optimization_barrier(
        (sent, rot_dest, block_order, ball_sizes, fine_qkv, fine_out, fine_gain)
    )
    targets, place = tables_of(rot_dest)
    members, lengths = ball_table(block_order[0], ball_sizes[0], crows // CBLK)
    gains = [fine_gain[j : j + 1] for j in range(3)]
    turned = [
        jnp.concatenate([w[:, :width].T, w[:, 2 * width :].T], axis=0) for w in (fine_qkv[1], fine_qkv[2])
    ]
    keys = [w[:, width : 2 * width] for w in (fine_qkv[1], fine_qkv[2])]

    arrived = exchange(sent)
    second, pieces = call(
        second_kernel,
        (shaped(BALLS, BALL, width), shaped(SUBS, POOL, CWIDTH)),
        [wide] + FINE_SCRATCH,
        (place, arrived, gains[1], turned[0], keys[0], fine_out[1], pool_weight),
        name="second_layer",
        **cost,
    )
    pieces = exchange(pieces)
    up = [(i, (i + 1) % groups) for i in range(groups)]
    down = [(i, (i - 1) % groups) for i in range(groups)]
    half = SUBS // 2
    left_a = lax.ppermute(pieces[:half], "grp", up)
    right_b = lax.ppermute(pieces[half:], "grp", down)
    left_b = lax.ppermute(pieces[half:], "grp", up)
    right_a = lax.ppermute(pieces[:half], "grp", down)
    gain = coarse_gain[None]
    pooled, own = call(
        own_kernel,
        (shaped(crows, CWIDTH), shaped(crows, 3 * CWIDTH)),
        [],
        (targets, pieces, gain, coarse_qkv),
        flops=2 * crows * CWIDTH * 3 * CWIDTH,
        name="own_projection",
    )
    far_a = lax.ppermute(left_a, "grp", up)
    far_b = lax.ppermute(right_b, "grp", down)
    left, right = call(
        near_kernel,
        (shaped(crows, 2 * CWIDTH), shaped(crows, 2 * CWIDTH)),
        [VM((SUBS, POOL, CWIDTH), BF16)],
        (targets, left_a, left_b, right_a, right_b, gain, coarse_qkv),
        flops=8 * crows * CWIDTH * CWIDTH,
        name="near_projection",
    )
    coarse, pieces = call(
        coarse_kernel,
        (shaped(crows, CWIDTH), shaped(SUBS, POOL, CWIDTH)),
        [
            VM((groups * crows, 2 * CWIDTH), BF16),
            VM((SUBS, POOL, CWIDTH), BF16),
            VM((crows, CWIDTH), BF16),
            VM((4 * CBLK, MOST_BALL * CBLK), F32),
            VM((4 * CBLK, MOST_BALL * CBLK), F32),
        ],
        (targets, members, lengths, pooled, own, left, right, far_a, far_b, gain, coarse_qkv, coarse_out),
        tables=3,
        flops=4 * 10**9,
        exps=2 * 10**6,
        name="coarse_layer",
        grant=24,
    )
    pieces = exchange(pieces)
    sent = call(
        third_kernel,
        shaped(SUBS, SUB, width),
        [wide, VM((BALLS, BALL, width), BF16)] + FINE_SCRATCH,
        (place, second, pieces, gains[2], turned[1], keys[1], fine_out[2], unpool_weight),
        name="third_layer",
        **cost,
    )
    mine = lax.dynamic_index_in_dim(targets, lax.axis_index("grp"), 0, False)
    refined = exchange(sent).at[mine].get(mode="promise_in_bounds", unique_indices=True)
    return refined.reshape(rows, width), coarse


def solution(mesh):
    return jax.shard_map(
        body,
        mesh=mesh,
        in_specs=(
            P(("pts", "grp"), None),
            P(),
            P("pts", None),
            P("pts", None),
            P(),
            P(),
            P(),
            P(),
            P(),
            P(),
            P(),
            P(),
        ),
        out_specs=(P(("pts", "grp"), None), P(("pts", "grp"), None)),
        check_vma=False,
    )
```

```python
import functools
import math

import jax
import jax.numpy as jnp
from jax import lax
from jax.experimental import pallas as pl
from jax.experimental.pallas import tpu as pltpu
from jax.sharding import PartitionSpec as P

F32, BF16 = jnp.float32, jnp.bfloat16
HEADS = 8
BALL = 256
SUB = 64
CBLK = 64
MOST_BALL = 8
WIDTH = 256
CWIDTH = 512
SUBS = 32
POOL = 16
LOG2E = 1.4426950408889634
NT = (((1,), (1,)), ((), ()))
TN = (((0,), (0,)), ((), ()))
VMEM = pl.BlockSpec(memory_space=pltpu.VMEM)
SMEM = pl.BlockSpec(memory_space=pltpu.SMEM)


def dot(a, b, dims=None):
    if dims is None:
        return jnp.dot(a, b, preferred_element_type=F32)
    return lax.dot_general(a, b, dims, preferred_element_type=F32)


def norm(x, gain):
    return (x * lax.rsqrt(jnp.mean(x * x, axis=-1, keepdims=True) + 1e-6) * gain).astype(BF16)


def head_masks():
    lane = lax.broadcasted_iota(jnp.int32, (1, 128), 1) // 32
    return [(lane == i).astype(F32).astype(BF16) for i in range(4)]


SCALE = LOG2E / math.sqrt(32.0)
BALLS = SUBS // 4
VM = pltpu.VMEM
HBM = pl.BlockSpec(memory_space=pltpu.HBM)


def transposed(wqkv_ref, wqvt_ref):
    wqvt_ref[:WIDTH] = wqkv_ref[:, :WIDTH].T
    wqvt_ref[WIDTH:] = wqkv_ref[:, 2 * WIDTH :].T


def fine_layer(load, reload, store, send, gain, wqvt_ref, wk_ref, wo_ref, scores, bufs, ready=None):
    left, right = scores
    k_s, qt_s, vt_s, ot_s = bufs[0:2], bufs[2:4], bufs[4:6], bufs[6:8]
    masks = head_masks()
    ones = jnp.ones((16, BALL), BF16)

    def project(b, par):
        h = norm(load(b), gain)
        qv = dot(wqvt_ref[...], h, NT)
        qt_s[par][...] = (qv[:WIDTH] * SCALE).astype(BF16)
        vt_s[par][...] = qv[WIDTH:].astype(BF16)
        k_s[par][...] = dot(h, wk_ref[...]).astype(BF16)

    def score(dst, par, g, i):
        keys = k_s[par][:, 128 * g : 128 * g + 128] * masks[i]
        dst[BALL * i : BALL * (i + 1)] = dot(keys, qt_s[par][128 * g : 128 * g + 128, :])

    def soft(src, par, g, i):
        s = src[BALL * i : BALL * (i + 1)]
        p = jnp.exp2(s - jnp.max(s, axis=0, keepdims=True)).astype(BF16)
        at = 32 * (4 * g + i)
        o = dot(jnp.concatenate([vt_s[par][at : at + 32], ones], axis=0), p)
        ot_s[par][at : at + 32] = (o[:32] * (1.0 / o[32:33])).astype(BF16)

    def finish(b, par):
        store(b, (reload(b) + dot(ot_s[par][...], wo_ref[...], TN)).astype(BF16))

    ot_s[1][...] = jnp.zeros_like(ot_s[1])
    project(0, 0)
    for i in range(4):
        score(left, 0, 0, i)
    if ready is not None:
        ready()

    def step(b, par):
        project(jnp.minimum(b + 1, BALLS - 1), 1 - par)
        for i in range(4):
            score(right, par, 1, i)
            soft(left, par, 0, i)
        finish(jnp.maximum(b - 1, 0), 1 - par)
        for i in range(4):
            score(left, 1 - par, 0, i)
            soft(right, par, 1, i)

    def pair(t, carry):
        if send is not None:

            @pl.when(t >= 1)
            def _():
                send(2 * t - 2)

            @pl.when(t >= 2)
            def _():
                send(2 * t - 3)

        step(2 * t, 0)
        step(2 * t + 1, 1)
        return carry

    lax.fori_loop(0, BALLS // 2, pair, 0)
    if send is not None:
        send(BALLS - 3)
        send(BALLS - 2)
    finish(BALLS - 1, 1)
    if send is not None:
        send(BALLS - 1)


def sent_to(staged, out, sem, at, to):
    pltpu.make_async_copy(staged.at[at], out.at[to], sem).start()


def all_sent(staged, out, sem):
    pltpu.make_async_copy(staged, out, sem).wait()


FINE_SCRATCH = [VM((4 * BALL, BALL), F32)] * 2 + [VM((BALL, WIDTH), BF16)] * 8


def first_kernel(
    rot_hbm, gain_hbm, x_hbm, wqkv_hbm, wo_hbm, out_hbm,
    rot, gain_ref, wqvt_ref, x_ref, wqkv_ref, wo_ref, staged, sems, *scratch
):
    groups = lax.axis_size("grp")
    device = lax.axis_index("pts") * groups + lax.axis_index("grp")
    weights = pltpu.make_async_copy(wqkv_hbm.at[0], wqkv_ref, sems.at[0])
    early = pltpu.make_async_copy(x_hbm.at[pl.ds(0, 4)], x_ref.at[pl.ds(0, 4)], sems.at[1])
    gains = pltpu.make_async_copy(gain_hbm, gain_ref, sems.at[2])
    late = [
        pltpu.make_async_copy(x_hbm.at[pl.ds(4, SUBS - 4)], x_ref.at[pl.ds(4, SUBS - 4)], sems.at[3]),
        pltpu.make_async_copy(wo_hbm.at[0], wo_ref, sems.at[4]),
        pltpu.make_async_copy(rot_hbm, rot, sems.at[5]),
    ]
    weights.start()
    early.start()
    gains.start()
    weights.wait()
    for copy in late:
        copy.start()
    transposed(wqkv_ref, wqvt_ref)
    early.wait()
    gains.wait()

    def ready():
        for copy in late:
            copy.wait()

    def load(b):
        return x_ref[pl.ds(4 * b, 4)].reshape(BALL, WIDTH).astype(F32)

    def store(b, y):
        staged[pl.ds(4 * b, 4)] = y.reshape(4, SUB, WIDTH)

    def send(b):
        for i in range(4):
            to = rot[device * SUBS + 4 * b + i] // (SUBS * groups)
            sent_to(staged, out_hbm, sems.at[6], 4 * b + i, to)

    wk_ref = wqkv_ref.at[:, WIDTH : 2 * WIDTH]
    fine_layer(
        load, load, store, send, gain_ref[0:1], wqvt_ref, wk_ref, wo_ref, scratch[:2], scratch[2:], ready
    )
    all_sent(staged, out_hbm, sems.at[6])


def second_kernel(
    place, x_ref, gain_ref, wqkv_ref, wo_ref, pool_ref, out_ref, pooled_ref, wqvt_ref, wide_ref, *scratch
):
    transposed(wqkv_ref, wqvt_ref)
    wk_ref = wqkv_ref.at[:, WIDTH : 2 * WIDTH]

    def load(b):
        return jnp.concatenate([x_ref[place[4 * b + i]] for i in range(4)], axis=0).astype(F32)

    def store(b, y):
        out_ref[b] = y
        wide = y.astype(F32)
        for c in range(2):
            wide_ref[c] = wide[:, 128 * c : 128 * c + 128]
        rows = jnp.concatenate(
            [wide_ref[c, pl.ds(j, BALL // 4, stride=4)] for j in range(4) for c in range(2)],
            axis=1,
        ).astype(BF16)
        pooled = dot(rows, pool_ref[...]).astype(BF16)
        for i in range(4):
            pooled_ref[place[4 * b + i]] = pooled[POOL * i : POOL * (i + 1)]

    fine_layer(
        load, load, store, None, gain_ref[1:2], wqvt_ref, wk_ref, wo_ref, scratch[:2], scratch[2:]
    )


def third_kernel(
    place, x_ref, coarse_ref, gain_ref, wqkv_ref, wo_ref, unpool_ref, out_ref,
    wqvt_ref, wide_ref, held_ref, *scratch
):
    transposed(wqkv_ref, wqvt_ref)
    wk_ref = wqkv_ref.at[:, WIDTH : 2 * WIDTH]

    def load(b):
        coarse = jnp.concatenate([coarse_ref[place[4 * b + i]] for i in range(4)], axis=0)
        lifted = dot(coarse, unpool_ref[...])
        for j in range(4):
            for c in range(2):
                at = WIDTH * j + 128 * c
                wide_ref[c, pl.ds(j, BALL // 4, stride=4)] = lifted[:, at : at + 128]
        x = x_ref[b].astype(F32) + jnp.concatenate([wide_ref[0], wide_ref[1]], axis=1)
        held_ref[b] = x.astype(BF16)
        return x.astype(BF16).astype(F32)

    def reload(b):
        return held_ref[b].astype(F32)

    def store(b, y):
        for i in range(4):
            out_ref[place[4 * b + i]] = y[SUB * i : SUB * (i + 1)]

    fine_layer(
        load, reload, store, None, gain_ref[2:3], wqvt_ref, wk_ref, wo_ref, scratch[:2], scratch[2:]
    )


def ordered_kernel(table, x_ref, out_hbm, sem):
    me = lax.axis_index("grp")
    for s in range(SUBS):
        sent_to(x_ref, out_hbm, sem, table[me, s], s)
    all_sent(x_ref, out_hbm, sem)


def group_of(step):
    return lax.rem(lax.axis_index("grp") + step, lax.axis_size("grp"))


def tree_rows(pieces, table, group):
    return jnp.concatenate([pieces(table[group, s]) for s in range(SUBS)], axis=0)


def own_kernel(table, pieces_ref, gain_ref, w_ref, pooled_ref, out_ref):
    pooled_ref[...] = tree_rows(lambda k: pieces_ref[k], table, group_of(0))
    out_ref[...] = dot(norm(pooled_ref[...].astype(F32), gain_ref[...]), w_ref[...]).astype(BF16)


def near_kernel(table, la_ref, lb_ref, ra_ref, rb_ref, gain_ref, w_ref, left_ref, right_ref, all_ref):
    groups = lax.axis_size("grp")
    half = SUBS // 2
    for step, a_ref, b_ref, out_ref in ((groups - 1, la_ref, lb_ref, left_ref), (1, ra_ref, rb_ref, right_ref)):
        all_ref[:half] = a_ref[...]
        all_ref[half:] = b_ref[...]
        rows = tree_rows(lambda k: all_ref[k], table, group_of(step)).astype(F32)
        out_ref[...] = dot(norm(rows, gain_ref[...]), w_ref[:, CWIDTH:]).astype(BF16)


def coarse_kernel(
    table, blocks, counts, pooled_ref, own_ref, left_ref, right_ref, far_a_ref, far_b_ref,
    gain_ref, w_ref, wo_ref, coarse_hbm, sent_hbm, kv_ref, all_ref, att_ref, a_ref, b_ref, staged, sems,
):
    groups = lax.axis_size("grp")
    me = lax.axis_index("grp")
    rows = CWIDTH
    half = SUBS // 2
    all_ref[:half] = far_a_ref[...]
    all_ref[half:] = far_b_ref[...]
    far = norm(tree_rows(lambda k: all_ref[k], table, group_of(2)).astype(F32), gain_ref[...])
    at = pl.multiple_of(group_of(2) * rows, rows)
    kv_ref[pl.ds(at, rows)] = dot(far, w_ref[:, CWIDTH:]).astype(BF16)
    for step, ref in ((0, own_ref), (groups - 1, left_ref), (1, right_ref)):
        at = pl.multiple_of(group_of(step) * rows, rows)
        kv_ref[pl.ds(at, rows)] = ref[:, ref.shape[1] - 2 * CWIDTH :]
    size = 64
    lanes = lax.broadcasted_iota(jnp.int32, (1, 256), 1) // size
    keep = [(lanes == i).astype(F32) for i in range(4)]
    keep_low = [m.astype(BF16) for m in keep]
    member = lax.broadcasted_iota(jnp.int32, (1, MOST_BALL * CBLK), 1) // CBLK

    def members(b, at):
        starts = [pl.multiple_of(blocks[b * MOST_BALL + m] * CBLK, CBLK) for m in range(MOST_BALL)]
        return jnp.concatenate([kv_ref[pl.ds(s, CBLK), at : at + 256] for s in starts], axis=0)

    def score(dst, b, g):
        q = own_ref[pl.ds(pl.multiple_of(b * CBLK, CBLK), CBLK), 256 * g : 256 * g + 256]
        spread = jnp.concatenate([q * keep_low[i] for i in range(4)], axis=0)
        scores = dot(spread, members(b, 256 * g), NT) * (LOG2E / 8.0)
        dst[...] = jnp.where(member < counts[b], scores, -jnp.inf)

    def soft(src, b, g):
        scores = src[...]
        expo = jnp.exp2(scores - jnp.max(scores, axis=-1, keepdims=True))
        scale = 1.0 / jnp.sum(expo, axis=-1, keepdims=True)
        out = dot(expo.astype(BF16), members(b, CWIDTH + 256 * g)) * scale
        total = sum(out[CBLK * i : CBLK * (i + 1)] * keep[i] for i in range(4))
        begin = pl.multiple_of(b * CBLK, CBLK)
        att_ref[pl.ds(begin, CBLK), 256 * g : 256 * g + 256] = total.astype(BF16)

    count = rows // CBLK
    score(a_ref, 0, 0)

    def block(b, carry):
        score(b_ref, b, 1)
        soft(a_ref, b, 0)
        score(a_ref, jnp.minimum(b + 1, count - 1), 0)
        soft(b_ref, b, 1)
        return carry

    lax.fori_loop(0, count, block, 0, unroll=2)
    part = SUBS // 4
    for c in range(4):
        at = slice(part * POOL * c, part * POOL * (c + 1))
        result = pooled_ref[at].astype(F32) + dot(att_ref[at], wo_ref[...])
        staged[part * c : part * (c + 1)] = result.astype(BF16).reshape(part, POOL, CWIDTH)
        near = pl.ds(part * c, part)
        pltpu.make_async_copy(staged.at[near], coarse_hbm.at[near], sems.at[0]).start()
        for s in range(part * c, part * (c + 1)):
            sent_to(staged, sent_hbm, sems.at[1], s, table[me, s])
    all_sent(staged, coarse_hbm, sems.at[0])
    all_sent(staged, sent_hbm, sems.at[1])


def call(kernel, outs, scratch, args, tables=1, flops=0, exps=0, name=None, grant=16, specs=None, out_specs=None):
    size = sum(a.size * a.dtype.itemsize for a in args)
    return pl.pallas_call(
        kernel,
        out_shape=outs,
        in_specs=specs or [SMEM] * tables + [VMEM] * (len(args) - tables),
        out_specs=jax.tree.map(lambda _: out_specs or VMEM, outs),
        scratch_shapes=scratch,
        name=name,
        compiler_params=pltpu.CompilerParams(vmem_limit_bytes=grant << 20),
        cost_estimate=pl.CostEstimate(flops=flops, bytes_accessed=2 * size, transcendentals=exps),
    )(*args)


def shaped(*shape):
    return jax.ShapeDtypeStruct(shape, BF16)


def exchange(pieces):
    return lax.all_to_all(pieces, "pts", split_axis=0, concat_axis=0, tiled=True)


def tables_of(rot_dest):
    points, groups = lax.axis_size("pts"), lax.axis_size("grp")
    point, group = lax.axis_index("pts"), lax.axis_index("grp")
    device = point * groups + group
    local = lax.dynamic_slice_in_dim(rot_dest, point * groups * SUBS, groups * SUBS)
    targets = (local // SUBS // groups).reshape(groups, SUBS)
    mine = lax.dynamic_index_in_dim(rot_dest.reshape(points, groups, SUBS), group, 1, False)
    slot = mine - device * SUBS
    source = jnp.arange(points, dtype=jnp.int32)
    hit = slot[None] == jnp.arange(SUBS, dtype=jnp.int32)[:, None, None]
    place = jnp.sum(jnp.where(hit, source[None, :, None], 0), axis=(1, 2))
    return targets, place.astype(jnp.int32)


def ball_table(order, sizes, count):
    total = order.shape[0]
    before = jnp.arange(sizes.shape[0])
    ends = jnp.sum(jnp.where(before[None, :] <= before[:, None], sizes[None, :], 0), axis=1)
    starts = ends - sizes
    marks = jnp.arange(total, dtype=jnp.int32)
    mine = lax.axis_index("grp") * count + jnp.arange(count, dtype=jnp.int32)
    where = jnp.sum(jnp.where(order[None, :] == mine[:, None], marks[None, :], 0), axis=1)
    inside = (starts[None, :] <= where[:, None]) & (where[:, None] < ends[None, :])
    first = jnp.sum(jnp.where(inside, starts[None, :], 0), axis=1)
    length = jnp.sum(jnp.where(inside, sizes[None, :], 0), axis=1)
    slots = jnp.arange(MOST_BALL, dtype=jnp.int32)
    place = jnp.minimum(first[:, None] + slots[None, :], total - 1)
    members = jnp.sum(
        jnp.where(place[:, :, None] == marks[None, None, :], order[None, None, :], 0), axis=2
    )
    return members.reshape(-1).astype(jnp.int32), length.astype(jnp.int32)


def body(
    points,
    rot_dest,
    block_order,
    ball_sizes,
    fine_gain,
    fine_qkv,
    fine_out,
    pool_weight,
    coarse_gain,
    coarse_qkv,
    coarse_out,
    unpool_weight,
):
    rows, width = points.shape
    groups = lax.axis_size("grp")
    crows = rows // 4
    wide = VM((2, BALL, 128), F32)
    cost = dict(flops=5 * 10**9, exps=4 * 10**6)
    sent = call(
        first_kernel,
        shaped(SUBS, SUB, width),
        [
            pltpu.SMEM(rot_dest.shape, jnp.int32),
            VM(fine_gain.shape, F32),
            VM((2 * width, width), BF16),
            VM((SUBS, SUB, width), BF16),
            VM((width, 3 * width), BF16),
            VM((width, width), BF16),
            VM((SUBS, SUB, width), BF16),
            pltpu.SemaphoreType.DMA((7,)),
        ]
        + FINE_SCRATCH,
        (rot_dest, fine_gain, points.reshape(SUBS, SUB, width), fine_qkv, fine_out),
        specs=[HBM] * 5,
        out_specs=HBM,
        name="first_layer",
        grant=60,
        **cost,
    )
    sent, rot_dest, block_order, ball_sizes, fine_qkv, fine_out, fine_gain = lax.optimization_barrier(
        (sent, rot_dest, block_order, ball_sizes, fine_qkv, fine_out, fine_gain)
    )
    targets, place = tables_of(rot_dest)
    members, lengths = ball_table(block_order[0], ball_sizes[0], crows // CBLK)
    packed = [fine_qkv[1], fine_qkv[2]]
    outer = [fine_out[1], fine_out[2]]

    arrived = exchange(sent)
    arrived, targets, place, members, lengths, packed, outer = lax.optimization_barrier(
        (arrived, targets, place, members, lengths, packed, outer)
    )
    second, pieces = call(
        second_kernel,
        (shaped(BALLS, BALL, width), shaped(SUBS, POOL, CWIDTH)),
        [VM((2 * width, width), BF16), wide] + FINE_SCRATCH,
        (place, arrived, fine_gain, packed[0], outer[0], pool_weight),
        name="second_layer",
        **cost,
    )
    pieces = exchange(pieces)
    up = [(i, (i + 1) % groups) for i in range(groups)]
    down = [(i, (i - 1) % groups) for i in range(groups)]
    half = SUBS // 2
    left_a = lax.ppermute(pieces[:half], "grp", up)
    right_b = lax.ppermute(pieces[half:], "grp", down)
    left_b = lax.ppermute(pieces[half:], "grp", up)
    right_a = lax.ppermute(pieces[:half], "grp", down)
    gain = coarse_gain[None]
    pooled, own = call(
        own_kernel,
        (shaped(crows, CWIDTH), shaped(crows, 3 * CWIDTH)),
        [],
        (targets, pieces, gain, coarse_qkv),
        flops=2 * crows * CWIDTH * 3 * CWIDTH,
        name="own_projection",
    )
    far_a = lax.ppermute(left_a, "grp", up)
    far_b = lax.ppermute(right_b, "grp", down)
    left, right = call(
        near_kernel,
        (shaped(crows, 2 * CWIDTH), shaped(crows, 2 * CWIDTH)),
        [VM((SUBS, POOL, CWIDTH), BF16)],
        (targets, left_a, left_b, right_a, right_b, gain, coarse_qkv),
        flops=8 * crows * CWIDTH * CWIDTH,
        name="near_projection",
    )
    coarse, pieces = call(
        coarse_kernel,
        (shaped(SUBS, POOL, CWIDTH), shaped(SUBS, POOL, CWIDTH)),
        [
            VM((groups * crows, 2 * CWIDTH), BF16),
            VM((SUBS, POOL, CWIDTH), BF16),
            VM((crows, CWIDTH), BF16),
            VM((4 * CBLK, MOST_BALL * CBLK), F32),
            VM((4 * CBLK, MOST_BALL * CBLK), F32),
            VM((SUBS, POOL, CWIDTH), BF16),
            pltpu.SemaphoreType.DMA((2,)),
        ],
        (targets, members, lengths, pooled, own, left, right, far_a, far_b, gain, coarse_qkv, coarse_out),
        tables=3,
        flops=4 * 10**9,
        exps=2 * 10**6,
        name="coarse_layer",
        out_specs=HBM,
        grant=24,
    )
    pieces = exchange(pieces)
    sent = call(
        third_kernel,
        shaped(SUBS, SUB, width),
        [VM((2 * width, width), BF16), wide, VM((BALLS, BALL, width), BF16)] + FINE_SCRATCH,
        (place, second, pieces, fine_gain, packed[1], outer[1], unpool_weight),
        name="third_layer",
        **cost,
    )
    refined = call(
        ordered_kernel,
        shaped(SUBS, SUB, width),
        [pltpu.SemaphoreType.DMA],
        (targets, exchange(sent)),
        out_specs=HBM,
        name="ordered",
    )
    return refined.reshape(rows, width), coarse.reshape(crows, CWIDTH)


def solution(mesh):
    return jax.shard_map(
        body,
        mesh=mesh,
        in_specs=(
            P(("pts", "grp"), None),
            P(),
            P("pts", None),
            P("pts", None),
            P(),
            P(),
            P(),
            P(),
            P(),
            P(),
            P(),
            P(),
        ),
        out_specs=(P(("pts", "grp"), None), P(("pts", "grp"), None)),
        check_vma=False,
    )
```

```python
import functools
import math

import jax
import jax.numpy as jnp
from jax import lax
from jax.experimental import pallas as pl
from jax.experimental.pallas import tpu as pltpu
from jax.sharding import PartitionSpec as P

F32, BF16 = jnp.float32, jnp.bfloat16
HEADS = 8
BALL = 256
SUB = 64
CBLK = 64
MOST_BALL = 8
WIDTH = 256
CWIDTH = 512
SUBS = 32
POOL = 16
LOG2E = 1.4426950408889634
NT = (((1,), (1,)), ((), ()))
TN = (((0,), (0,)), ((), ()))
VMEM = pl.BlockSpec(memory_space=pltpu.VMEM)
SMEM = pl.BlockSpec(memory_space=pltpu.SMEM)


def dot(a, b, dims=None):
    if dims is None:
        return jnp.dot(a, b, preferred_element_type=F32)
    return lax.dot_general(a, b, dims, preferred_element_type=F32)


def norm(x, gain):
    return (x * lax.rsqrt(jnp.mean(x * x, axis=-1, keepdims=True) + 1e-6) * gain).astype(BF16)


def head_masks():
    lane = lax.broadcasted_iota(jnp.int32, (1, 128), 1) // 32
    return [(lane == i).astype(F32).astype(BF16) for i in range(4)]


SCALE = LOG2E / math.sqrt(32.0)
BALLS = SUBS // 4
VM = pltpu.VMEM
HBM = pl.BlockSpec(memory_space=pltpu.HBM)


def transposed(wqkv_ref, wqvt_ref):
    wqvt_ref[:WIDTH] = wqkv_ref[:, :WIDTH].T
    wqvt_ref[WIDTH:] = wqkv_ref[:, 2 * WIDTH :].T


def fine_layer(load, reload, store, send, gain, wqvt_ref, wk_ref, wo_ref, scores, bufs, ready=None):
    left, right = scores
    k_s, qt_s, vt_s, ot_s = bufs[0:2], bufs[2:4], bufs[4:6], bufs[6:8]
    masks = head_masks()
    ones = jnp.ones((16, BALL), BF16)

    def project(b, par):
        h = norm(load(b), gain)
        qv = dot(wqvt_ref[...], h, NT)
        qt_s[par][...] = (qv[:WIDTH] * SCALE).astype(BF16)
        vt_s[par][...] = qv[WIDTH:].astype(BF16)
        k_s[par][...] = dot(h, wk_ref[...]).astype(BF16)

    def score(dst, par, g, i):
        keys = k_s[par][:, 128 * g : 128 * g + 128] * masks[i]
        dst[BALL * i : BALL * (i + 1)] = dot(keys, qt_s[par][128 * g : 128 * g + 128, :])

    def soft(src, par, g, i):
        s = src[BALL * i : BALL * (i + 1)]
        p = jnp.exp2(s - jnp.max(s, axis=0, keepdims=True)).astype(BF16)
        at = 32 * (4 * g + i)
        o = dot(jnp.concatenate([vt_s[par][at : at + 32], ones], axis=0), p)
        ot_s[par][at : at + 32] = (o[:32] * (1.0 / o[32:33])).astype(BF16)

    def finish(b, par):
        store(b, (reload(b) + dot(ot_s[par][...], wo_ref[...], TN)).astype(BF16))

    ot_s[1][...] = jnp.zeros_like(ot_s[1])
    project(0, 0)
    for i in range(4):
        score(left, 0, 0, i)
    if ready is not None:
        ready()

    def step(b, par):
        project(jnp.minimum(b + 1, BALLS - 1), 1 - par)
        for i in range(4):
            score(right, par, 1, i)
            soft(left, par, 0, i)
        finish(jnp.maximum(b - 1, 0), 1 - par)
        for i in range(4):
            score(left, 1 - par, 0, i)
            soft(right, par, 1, i)

    def pair(t, carry):
        if send is not None:

            @pl.when(t >= 1)
            def _():
                send(2 * t - 2)

            @pl.when(t >= 2)
            def _():
                send(2 * t - 3)

        step(2 * t, 0)
        step(2 * t + 1, 1)
        return carry

    lax.fori_loop(0, BALLS // 2, pair, 0)
    if send is not None:
        send(BALLS - 3)
        send(BALLS - 2)
    finish(BALLS - 1, 1)
    if send is not None:
        send(BALLS - 1)


def sent_to(staged, out, sem, at, to):
    pltpu.make_async_copy(staged.at[at], out.at[to], sem).start()


def all_sent(staged, out, sem):
    pltpu.make_async_copy(staged, out, sem).wait()


FINE_SCRATCH = [VM((4 * BALL, BALL), F32)] * 2 + [VM((BALL, WIDTH), BF16)] * 8


def first_kernel(
    rot_hbm, gain_hbm, x_hbm, wqkv_hbm, wo_hbm, out_hbm,
    rot, gain_ref, wqvt_ref, x_ref, wqkv_ref, wo_ref, staged, sems, *scratch
):
    groups = lax.axis_size("grp")
    device = lax.axis_index("pts") * groups + lax.axis_index("grp")
    weights = pltpu.make_async_copy(wqkv_hbm.at[0], wqkv_ref, sems.at[0])
    early = pltpu.make_async_copy(x_hbm.at[pl.ds(0, 4)], x_ref.at[pl.ds(0, 4)], sems.at[1])
    gains = pltpu.make_async_copy(gain_hbm, gain_ref, sems.at[2])
    late = [
        pltpu.make_async_copy(x_hbm.at[pl.ds(4, SUBS - 4)], x_ref.at[pl.ds(4, SUBS - 4)], sems.at[3]),
        pltpu.make_async_copy(wo_hbm.at[0], wo_ref, sems.at[4]),
        pltpu.make_async_copy(rot_hbm, rot, sems.at[5]),
    ]
    weights.start()
    early.start()
    gains.start()
    weights.wait()
    for copy in late:
        copy.start()
    transposed(wqkv_ref, wqvt_ref)
    early.wait()
    gains.wait()

    def ready():
        for copy in late:
            copy.wait()

    def load(b):
        return x_ref[pl.ds(4 * b, 4)].reshape(BALL, WIDTH).astype(F32)

    def store(b, y):
        staged[pl.ds(4 * b, 4)] = y.reshape(4, SUB, WIDTH)

    def send(b):
        for i in range(4):
            to = rot[device * SUBS + 4 * b + i] // (SUBS * groups)
            sent_to(staged, out_hbm, sems.at[6], 4 * b + i, to)

    wk_ref = wqkv_ref.at[:, WIDTH : 2 * WIDTH]
    fine_layer(
        load, load, store, send, gain_ref[0:1], wqvt_ref, wk_ref, wo_ref, scratch[:2], scratch[2:], ready
    )
    all_sent(staged, out_hbm, sems.at[6])


def second_kernel(
    place, x_ref, gain_ref, wqkv_ref, wo_ref, pool_ref, out_ref, pooled_ref, wqvt_ref, wide_ref, rows_ref, *scratch
):
    transposed(wqkv_ref, wqvt_ref)
    wk_ref = wqkv_ref.at[:, WIDTH : 2 * WIDTH]

    def load(b):
        return jnp.concatenate([x_ref[place[4 * b + i]] for i in range(4)], axis=0).astype(F32)

    def store(b, y):
        out_ref[b] = y
        wide = y.astype(F32)
        for c in range(2):
            wide_ref[c] = wide[:, 128 * c : 128 * c + 128]
        rows_ref[b] = jnp.concatenate(
            [wide_ref[c, pl.ds(j, BALL // 4, stride=4)] for j in range(4) for c in range(2)],
            axis=1,
        ).astype(BF16)

    fine_layer(
        load, load, store, None, gain_ref[1:2], wqvt_ref, wk_ref, wo_ref, scratch[:2], scratch[2:]
    )
    part = BALLS // 2
    for b in range(0, BALLS, part):
        rows = rows_ref[b : b + part].reshape(part * BALL // 4, 4 * WIDTH)
        pooled = dot(rows, pool_ref[...]).astype(BF16)
        for i in range(4 * part):
            pooled_ref[place[4 * b + i]] = pooled[POOL * i : POOL * (i + 1)]


def third_kernel(
    place, x_ref, coarse_ref, gain_ref, wqkv_ref, wo_ref, unpool_ref, out_ref,
    wqvt_ref, wide_ref, lifted_ref, held_ref, *scratch
):
    transposed(wqkv_ref, wqvt_ref)
    wk_ref = wqkv_ref.at[:, WIDTH : 2 * WIDTH]

    part = BALLS // 2
    for b in range(0, BALLS, part):
        coarse = jnp.concatenate([coarse_ref[place[4 * b + i]] for i in range(4 * part)], axis=0)
        lifted_ref[b : b + part] = dot(coarse, unpool_ref[...]).reshape(part, BALL // 4, 4 * WIDTH)

    def load(b):
        for j in range(4):
            for c in range(2):
                at = WIDTH * j + 128 * c
                wide_ref[c, pl.ds(j, BALL // 4, stride=4)] = lifted_ref[b, :, at : at + 128]
        x = x_ref[b].astype(F32) + jnp.concatenate([wide_ref[0], wide_ref[1]], axis=1)
        held_ref[b] = x.astype(BF16)
        return x.astype(BF16).astype(F32)

    def reload(b):
        return held_ref[b].astype(F32)

    def store(b, y):
        for i in range(4):
            out_ref[place[4 * b + i]] = y[SUB * i : SUB * (i + 1)]

    fine_layer(
        load, reload, store, None, gain_ref[2:3], wqvt_ref, wk_ref, wo_ref, scratch[:2], scratch[2:]
    )


def ordered_kernel(table, x_ref, out_hbm, sem):
    me = lax.axis_index("grp")
    for s in range(SUBS):
        sent_to(x_ref, out_hbm, sem, table[me, s], s)
    all_sent(x_ref, out_hbm, sem)


def group_of(step):
    return lax.rem(lax.axis_index("grp") + step, lax.axis_size("grp"))


def tree_rows(pieces, table, group):
    return jnp.concatenate([pieces(table[group, s]) for s in range(SUBS)], axis=0)


def own_kernel(table, pieces_ref, gain_ref, w_ref, pooled_ref, out_ref):
    pooled_ref[...] = tree_rows(lambda k: pieces_ref[k], table, group_of(0))
    out_ref[...] = dot(norm(pooled_ref[...].astype(F32), gain_ref[...]), w_ref[...]).astype(BF16)


def near_kernel(table, la_ref, lb_ref, ra_ref, rb_ref, gain_ref, w_ref, left_ref, right_ref, all_ref):
    groups = lax.axis_size("grp")
    half = SUBS // 2
    for step, a_ref, b_ref, out_ref in ((groups - 1, la_ref, lb_ref, left_ref), (1, ra_ref, rb_ref, right_ref)):
        all_ref[:half] = a_ref[...]
        all_ref[half:] = b_ref[...]
        rows = tree_rows(lambda k: all_ref[k], table, group_of(step)).astype(F32)
        out_ref[...] = dot(norm(rows, gain_ref[...]), w_ref[:, CWIDTH:]).astype(BF16)


def coarse_kernel(
    table, blocks, counts, pooled_ref, own_ref, left_ref, right_ref, far_a_ref, far_b_ref,
    gain_ref, w_ref, wo_ref, coarse_hbm, sent_ref, kv_ref, all_ref, att_ref, a_ref, b_ref, staged, sem,
):
    groups = lax.axis_size("grp")
    me = lax.axis_index("grp")
    rows = CWIDTH
    half = SUBS // 2
    all_ref[:half] = far_a_ref[...]
    all_ref[half:] = far_b_ref[...]
    far = norm(tree_rows(lambda k: all_ref[k], table, group_of(2)).astype(F32), gain_ref[...])
    at = pl.multiple_of(group_of(2) * rows, rows)
    kv_ref[pl.ds(at, rows)] = dot(far, w_ref[:, CWIDTH:]).astype(BF16)
    for step, ref in ((0, own_ref), (groups - 1, left_ref), (1, right_ref)):
        at = pl.multiple_of(group_of(step) * rows, rows)
        kv_ref[pl.ds(at, rows)] = ref[:, ref.shape[1] - 2 * CWIDTH :]
    size = 64
    lanes = lax.broadcasted_iota(jnp.int32, (1, 256), 1) // size
    keep = [(lanes == i).astype(F32) for i in range(4)]
    keep_low = [m.astype(BF16) for m in keep]
    member = lax.broadcasted_iota(jnp.int32, (1, MOST_BALL * CBLK), 1) // CBLK

    def members(b, at):
        starts = [pl.multiple_of(blocks[b * MOST_BALL + m] * CBLK, CBLK) for m in range(MOST_BALL)]
        return jnp.concatenate([kv_ref[pl.ds(s, CBLK), at : at + 256] for s in starts], axis=0)

    def score(dst, b, g):
        q = own_ref[pl.ds(pl.multiple_of(b * CBLK, CBLK), CBLK), 256 * g : 256 * g + 256]
        spread = jnp.concatenate([q * keep_low[i] for i in range(4)], axis=0)
        scores = dot(spread, members(b, 256 * g), NT) * (LOG2E / 8.0)
        dst[...] = jnp.where(member < counts[b], scores, -jnp.inf)

    def soft(src, b, g):
        scores = src[...]
        expo = jnp.exp2(scores - jnp.max(scores, axis=-1, keepdims=True))
        scale = 1.0 / jnp.sum(expo, axis=-1, keepdims=True)
        out = dot(expo.astype(BF16), members(b, CWIDTH + 256 * g)) * scale
        total = sum(out[CBLK * i : CBLK * (i + 1)] * keep[i] for i in range(4))
        begin = pl.multiple_of(b * CBLK, CBLK)
        att_ref[pl.ds(begin, CBLK), 256 * g : 256 * g + 256] = total.astype(BF16)

    count = rows // CBLK
    score(a_ref, 0, 0)

    def block(b, carry):
        score(b_ref, b, 1)
        soft(a_ref, b, 0)
        score(a_ref, jnp.minimum(b + 1, count - 1), 0)
        soft(b_ref, b, 1)
        return carry

    lax.fori_loop(0, count, block, 0, unroll=2)
    part = SUBS // 4
    for c in range(4):
        at = slice(part * POOL * c, part * POOL * (c + 1))
        result = pooled_ref[at].astype(F32) + dot(att_ref[at], wo_ref[...])
        result = result.astype(BF16).reshape(part, POOL, CWIDTH)
        staged[part * c : part * (c + 1)] = result
        near = pl.ds(part * c, part)
        pltpu.make_async_copy(staged.at[near], coarse_hbm.at[near], sem).start()
        for s in range(part):
            sent_ref[table[me, part * c + s]] = result[s]
    all_sent(staged, coarse_hbm, sem)


def call(kernel, outs, scratch, args, tables=1, flops=0, exps=0, name=None, grant=16, specs=None, out_specs=None):
    size = sum(a.size * a.dtype.itemsize for a in args)
    return pl.pallas_call(
        kernel,
        out_shape=outs,
        in_specs=specs or [SMEM] * tables + [VMEM] * (len(args) - tables),
        out_specs=out_specs if isinstance(out_specs, tuple) else jax.tree.map(lambda _: out_specs or VMEM, outs),
        scratch_shapes=scratch,
        name=name,
        compiler_params=pltpu.CompilerParams(vmem_limit_bytes=grant << 20),
        cost_estimate=pl.CostEstimate(flops=flops, bytes_accessed=2 * size, transcendentals=exps),
    )(*args)


def shaped(*shape):
    return jax.ShapeDtypeStruct(shape, BF16)


def exchange(pieces):
    return lax.all_to_all(pieces, "pts", split_axis=0, concat_axis=0, tiled=True)


def tables_of(rot_dest):
    points, groups = lax.axis_size("pts"), lax.axis_size("grp")
    point, group = lax.axis_index("pts"), lax.axis_index("grp")
    device = point * groups + group
    local = lax.dynamic_slice_in_dim(rot_dest, point * groups * SUBS, groups * SUBS)
    targets = (local // SUBS // groups).reshape(groups, SUBS)
    mine = lax.dynamic_index_in_dim(rot_dest.reshape(points, groups, SUBS), group, 1, False)
    slot = mine - device * SUBS
    source = jnp.arange(points, dtype=jnp.int32)
    hit = slot[None] == jnp.arange(SUBS, dtype=jnp.int32)[:, None, None]
    place = jnp.sum(jnp.where(hit, source[None, :, None], 0), axis=(1, 2))
    return targets, place.astype(jnp.int32)


def ball_table(order, sizes, count):
    total = order.shape[0]
    before = jnp.arange(sizes.shape[0])
    ends = jnp.sum(jnp.where(before[None, :] <= before[:, None], sizes[None, :], 0), axis=1)
    starts = ends - sizes
    marks = jnp.arange(total, dtype=jnp.int32)
    mine = lax.axis_index("grp") * count + jnp.arange(count, dtype=jnp.int32)
    where = jnp.sum(jnp.where(order[None, :] == mine[:, None], marks[None, :], 0), axis=1)
    inside = (starts[None, :] <= where[:, None]) & (where[:, None] < ends[None, :])
    first = jnp.sum(jnp.where(inside, starts[None, :], 0), axis=1)
    length = jnp.sum(jnp.where(inside, sizes[None, :], 0), axis=1)
    slots = jnp.arange(MOST_BALL, dtype=jnp.int32)
    place = jnp.minimum(first[:, None] + slots[None, :], total - 1)
    members = jnp.sum(
        jnp.where(place[:, :, None] == marks[None, None, :], order[None, None, :], 0), axis=2
    )
    return members.reshape(-1).astype(jnp.int32), length.astype(jnp.int32)


def body(
    points,
    rot_dest,
    block_order,
    ball_sizes,
    fine_gain,
    fine_qkv,
    fine_out,
    pool_weight,
    coarse_gain,
    coarse_qkv,
    coarse_out,
    unpool_weight,
):
    rows, width = points.shape
    groups = lax.axis_size("grp")
    crows = rows // 4
    wide = VM((2, BALL, 128), F32)
    cost = dict(flops=5 * 10**9, exps=4 * 10**6)
    sent = call(
        first_kernel,
        shaped(SUBS, SUB, width),
        [
            pltpu.SMEM(rot_dest.shape, jnp.int32),
            VM(fine_gain.shape, F32),
            VM((2 * width, width), BF16),
            VM((SUBS, SUB, width), BF16),
            VM((width, 3 * width), BF16),
            VM((width, width), BF16),
            VM((SUBS, SUB, width), BF16),
            pltpu.SemaphoreType.DMA((7,)),
        ]
        + FINE_SCRATCH,
        (rot_dest, fine_gain, points.reshape(SUBS, SUB, width), fine_qkv, fine_out),
        specs=[HBM] * 5,
        out_specs=HBM,
        name="first_layer",
        grant=60,
        **cost,
    )
    sent, rot_dest, block_order, ball_sizes, fine_qkv, fine_out, fine_gain = lax.optimization_barrier(
        (sent, rot_dest, block_order, ball_sizes, fine_qkv, fine_out, fine_gain)
    )
    targets, place = tables_of(rot_dest)
    members, lengths = ball_table(block_order[0], ball_sizes[0], crows // CBLK)
    packed = [fine_qkv[1], fine_qkv[2]]
    outer = [fine_out[1], fine_out[2]]

    arrived = exchange(sent)
    arrived, targets, place, members, lengths, packed, outer = lax.optimization_barrier(
        (arrived, targets, place, members, lengths, packed, outer)
    )
    second, pieces = call(
        second_kernel,
        (shaped(BALLS, BALL, width), shaped(SUBS, POOL, CWIDTH)),
        [VM((2 * width, width), BF16), wide, VM((BALLS, BALL // 4, 4 * width), BF16)] + FINE_SCRATCH,
        (place, arrived, fine_gain, packed[0], outer[0], pool_weight),
        name="second_layer",
        **cost,
    )
    pieces = exchange(pieces)
    up = [(i, (i + 1) % groups) for i in range(groups)]
    down = [(i, (i - 1) % groups) for i in range(groups)]
    half = SUBS // 2
    left_a = lax.ppermute(pieces[:half], "grp", up)
    right_b = lax.ppermute(pieces[half:], "grp", down)
    left_b = lax.ppermute(pieces[half:], "grp", up)
    right_a = lax.ppermute(pieces[:half], "grp", down)
    gain = coarse_gain[None]
    pooled, own = call(
        own_kernel,
        (shaped(crows, CWIDTH), shaped(crows, 3 * CWIDTH)),
        [],
        (targets, pieces, gain, coarse_qkv),
        flops=2 * crows * CWIDTH * 3 * CWIDTH,
        name="own_projection",
    )
    far_a = lax.ppermute(left_a, "grp", up)
    far_b = lax.ppermute(right_b, "grp", down)
    left, right = call(
        near_kernel,
        (shaped(crows, 2 * CWIDTH), shaped(crows, 2 * CWIDTH)),
        [VM((SUBS, POOL, CWIDTH), BF16)],
        (targets, left_a, left_b, right_a, right_b, gain, coarse_qkv),
        flops=8 * crows * CWIDTH * CWIDTH,
        name="near_projection",
    )
    coarse, pieces = call(
        coarse_kernel,
        (shaped(SUBS, POOL, CWIDTH), shaped(SUBS, POOL, CWIDTH)),
        [
            VM((groups * crows, 2 * CWIDTH), BF16),
            VM((SUBS, POOL, CWIDTH), BF16),
            VM((crows, CWIDTH), BF16),
            VM((4 * CBLK, MOST_BALL * CBLK), F32),
            VM((4 * CBLK, MOST_BALL * CBLK), F32),
            VM((SUBS, POOL, CWIDTH), BF16),
            pltpu.SemaphoreType.DMA,
        ],
        (targets, members, lengths, pooled, own, left, right, far_a, far_b, gain, coarse_qkv, coarse_out),
        tables=3,
        flops=4 * 10**9,
        exps=2 * 10**6,
        name="coarse_layer",
        out_specs=(HBM, VMEM),
        grant=24,
    )
    pieces = exchange(pieces)
    sent = call(
        third_kernel,
        shaped(SUBS, SUB, width),
        [
            VM((2 * width, width), BF16),
            wide,
            VM((BALLS, BALL // 4, 4 * width), F32),
            VM((BALLS, BALL, width), BF16),
        ]
        + FINE_SCRATCH,
        (place, second, pieces, fine_gain, packed[1], outer[1], unpool_weight),
        name="third_layer",
        **cost,
    )
    refined = call(
        ordered_kernel,
        shaped(SUBS, SUB, width),
        [pltpu.SemaphoreType.DMA],
        (targets, exchange(sent)),
        out_specs=HBM,
        name="ordered",
    )
    return refined.reshape(rows, width), coarse.reshape(crows, CWIDTH)


def solution(mesh):
    return jax.shard_map(
        body,
        mesh=mesh,
        in_specs=(
            P(("pts", "grp"), None),
            P(),
            P("pts", None),
            P("pts", None),
            P(),
            P(),
            P(),
            P(),
            P(),
            P(),
            P(),
            P(),
        ),
        out_specs=(P(("pts", "grp"), None), P(("pts", "grp"), None)),
        check_vma=False,
    )
```

```python
import functools
import math

import jax
import jax.numpy as jnp
from jax import lax
from jax.experimental import pallas as pl
from jax.experimental.pallas import tpu as pltpu
from jax.sharding import PartitionSpec as P

F32, BF16 = jnp.float32, jnp.bfloat16
HEADS = 8
BALL = 256
SUB = 64
CBLK = 64
MOST_BALL = 8
WIDTH = 256
CWIDTH = 512
SUBS = 32
POOL = 16
LOG2E = 1.4426950408889634
NT = (((1,), (1,)), ((), ()))
TN = (((0,), (0,)), ((), ()))
VMEM = pl.BlockSpec(memory_space=pltpu.VMEM)
SMEM = pl.BlockSpec(memory_space=pltpu.SMEM)


def dot(a, b, dims=None):
    if dims is None:
        return jnp.dot(a, b, preferred_element_type=F32)
    return lax.dot_general(a, b, dims, preferred_element_type=F32)


def norm(x, gain):
    return (x * lax.rsqrt(jnp.mean(x * x, axis=-1, keepdims=True) + 1e-6) * gain).astype(BF16)


SCALE = LOG2E / math.sqrt(32.0)
BALLS = SUBS // 4
VM = pltpu.VMEM
HBM = pl.BlockSpec(memory_space=pltpu.HBM)


def transposed(wqkv_ref, wqvt_ref):
    wqvt_ref[:WIDTH] = wqkv_ref[:, :WIDTH].T
    wqvt_ref[WIDTH:] = wqkv_ref[:, 2 * WIDTH :].T


def fine_layer(load, reload, store, send, gain, wqvt_ref, wk_ref, wo_ref, scores, bufs, ready=None):
    left, right = scores
    k_s, qt_s, vt_s, ot_s = bufs[0:2], bufs[2:4], bufs[4:6], bufs[6:8]
    ones = jnp.ones((16, BALL), BF16)

    def project(b, par):
        h = norm(load(b), gain)
        qv = dot(wqvt_ref[...], h, NT)
        qt_s[par][...] = (qv[:WIDTH] * SCALE).astype(BF16)
        vt_s[par][...] = qv[WIDTH:].astype(BF16)
        k_s[par][...] = dot(h, wk_ref[...]).astype(BF16)

    def score(dst, par, g, i):
        at = 32 * (4 * g + i)
        parts = [jnp.zeros((32 * i, BALL), BF16), qt_s[par][at : at + 32], jnp.zeros((96 - 32 * i, BALL), BF16)]
        query = jnp.concatenate([p for p in parts if p.shape[0]], axis=0)
        dst[BALL * i : BALL * (i + 1)] = dot(k_s[par][:, 128 * g : 128 * g + 128], query)

    def soft(src, par, g, i):
        s = src[BALL * i : BALL * (i + 1)]
        p = jnp.exp2(s - jnp.max(s, axis=0, keepdims=True)).astype(BF16)
        at = 32 * (4 * g + i)
        o = dot(jnp.concatenate([vt_s[par][at : at + 32], ones], axis=0), p)
        ot_s[par][at : at + 32] = (o[:32] * (1.0 / o[32:33])).astype(BF16)

    def finish(b, par):
        store(b, (reload(b) + dot(ot_s[par][...], wo_ref[...], TN)).astype(BF16))

    project(0, 0)
    for i in range(4):
        score(left, 0, 0, i)
    if ready is not None:
        ready()
    for b in range(BALLS):
        par, last = b % 2, b == BALLS - 1
        if send is not None and b % 2 == 0:
            for done in (b - 3, b - 2):
                if done >= 0:
                    send(done)
        if not last:
            project(b + 1, 1 - par)
        for i in range(4):
            score(right, par, 1, i)
            soft(left, par, 0, i)
        if b > 0:
            finish(b - 1, 1 - par)
        for i in range(4):
            if not last:
                score(left, 1 - par, 0, i)
            soft(right, par, 1, i)
    if send is not None:
        send(BALLS - 3)
        send(BALLS - 2)
    finish(BALLS - 1, (BALLS - 1) % 2)
    if send is not None:
        send(BALLS - 1)


def sent_to(staged, out, sem, at, to):
    pltpu.make_async_copy(staged.at[at], out.at[to], sem).start()


def all_sent(staged, out, sem):
    pltpu.make_async_copy(staged, out, sem).wait()


FINE_SCRATCH = [VM((4 * BALL, BALL), F32)] * 2 + [VM((BALL, WIDTH), BF16)] * 8


def first_kernel(
    rot_hbm, gain_hbm, x_hbm, wqkv_hbm, wo_hbm, out_hbm,
    rot, gain_ref, wqvt_ref, x_ref, wqkv_ref, wo_ref, staged, sems, *scratch
):
    groups = lax.axis_size("grp")
    device = lax.axis_index("pts") * groups + lax.axis_index("grp")
    weights = pltpu.make_async_copy(wqkv_hbm.at[0], wqkv_ref, sems.at[0])
    early = pltpu.make_async_copy(x_hbm.at[pl.ds(0, 4)], x_ref.at[pl.ds(0, 4)], sems.at[1])
    gains = pltpu.make_async_copy(gain_hbm, gain_ref, sems.at[2])
    late = [
        pltpu.make_async_copy(x_hbm.at[pl.ds(4, SUBS - 4)], x_ref.at[pl.ds(4, SUBS - 4)], sems.at[3]),
        pltpu.make_async_copy(wo_hbm.at[0], wo_ref, sems.at[4]),
        pltpu.make_async_copy(rot_hbm, rot, sems.at[5]),
    ]
    weights.start()
    early.start()
    gains.start()
    weights.wait()
    for copy in late:
        copy.start()
    transposed(wqkv_ref, wqvt_ref)
    early.wait()
    gains.wait()

    def ready():
        for copy in late:
            copy.wait()

    def load(b):
        return x_ref[pl.ds(4 * b, 4)].reshape(BALL, WIDTH).astype(F32)

    def store(b, y):
        staged[pl.ds(4 * b, 4)] = y.reshape(4, SUB, WIDTH)

    def send(b):
        for i in range(4):
            to = rot[device * SUBS + 4 * b + i] // (SUBS * groups)
            sent_to(staged, out_hbm, sems.at[6], 4 * b + i, to)

    wk_ref = wqkv_ref.at[:, WIDTH : 2 * WIDTH]
    fine_layer(
        load, load, store, send, gain_ref[0:1], wqvt_ref, wk_ref, wo_ref, scratch[:2], scratch[2:], ready
    )
    all_sent(staged, out_hbm, sems.at[6])


def second_kernel(
    place, x_ref, gain_ref, wqkv_ref, wo_ref, pool_ref, out_ref, pooled_ref, wqvt_ref, wide_ref, rows_ref, *scratch
):
    transposed(wqkv_ref, wqvt_ref)
    wk_ref = wqkv_ref.at[:, WIDTH : 2 * WIDTH]

    def load(b):
        return jnp.concatenate([x_ref[place[4 * b + i]] for i in range(4)], axis=0).astype(F32)

    def store(b, y):
        out_ref[b] = y
        wide = y.astype(F32)
        for c in range(2):
            wide_ref[c] = wide[:, 128 * c : 128 * c + 128]
        rows_ref[b] = jnp.concatenate(
            [wide_ref[c, pl.ds(j, BALL // 4, stride=4)] for j in range(4) for c in range(2)],
            axis=1,
        ).astype(BF16)

    fine_layer(
        load, load, store, None, gain_ref[1:2], wqvt_ref, wk_ref, wo_ref, scratch[:2], scratch[2:]
    )
    part = BALLS // 2
    for b in range(0, BALLS, part):
        rows = rows_ref[b : b + part].reshape(part * BALL // 4, 4 * WIDTH)
        pooled = dot(rows, pool_ref[...]).astype(BF16)
        for i in range(4 * part):
            pooled_ref[place[4 * b + i]] = pooled[POOL * i : POOL * (i + 1)]


def third_kernel(
    place, x_ref, coarse_ref, gain_ref, wqkv_ref, wo_ref, unpool_ref, out_ref,
    wqvt_ref, wide_ref, lifted_ref, held_ref, *scratch
):
    transposed(wqkv_ref, wqvt_ref)
    wk_ref = wqkv_ref.at[:, WIDTH : 2 * WIDTH]

    part = BALLS // 2
    for b in range(0, BALLS, part):
        coarse = jnp.concatenate([coarse_ref[place[4 * b + i]] for i in range(4 * part)], axis=0)
        lifted_ref[b : b + part] = dot(coarse, unpool_ref[...]).reshape(part, BALL // 4, 4 * WIDTH)

    def load(b):
        for j in range(4):
            for c in range(2):
                at = WIDTH * j + 128 * c
                wide_ref[c, pl.ds(j, BALL // 4, stride=4)] = lifted_ref[b, :, at : at + 128]
        x = x_ref[b].astype(F32) + jnp.concatenate([wide_ref[0], wide_ref[1]], axis=1)
        held_ref[b] = x.astype(BF16)
        return x.astype(BF16).astype(F32)

    def reload(b):
        return held_ref[b].astype(F32)

    def store(b, y):
        for i in range(4):
            out_ref[place[4 * b + i]] = y[SUB * i : SUB * (i + 1)]

    fine_layer(
        load, reload, store, None, gain_ref[2:3], wqvt_ref, wk_ref, wo_ref, scratch[:2], scratch[2:]
    )


def ordered_kernel(table, x_ref, out_hbm, sem):
    me = lax.axis_index("grp")
    for s in range(SUBS):
        sent_to(x_ref, out_hbm, sem, table[me, s], s)
    all_sent(x_ref, out_hbm, sem)


def group_of(step):
    return lax.rem(lax.axis_index("grp") + step, lax.axis_size("grp"))


def tree_rows(pieces, table, group):
    return jnp.concatenate([pieces(table[group, s]) for s in range(SUBS)], axis=0)


def own_kernel(table, pieces_ref, gain_ref, w_ref, pooled_ref, out_ref):
    pooled_ref[...] = tree_rows(lambda k: pieces_ref[k], table, group_of(0))
    out_ref[...] = dot(norm(pooled_ref[...].astype(F32), gain_ref[...]), w_ref[...]).astype(BF16)


def near_kernel(table, la_ref, lb_ref, ra_ref, rb_ref, gain_ref, w_ref, left_ref, right_ref, all_ref):
    groups = lax.axis_size("grp")
    half = SUBS // 2
    for step, a_ref, b_ref, out_ref in ((groups - 1, la_ref, lb_ref, left_ref), (1, ra_ref, rb_ref, right_ref)):
        all_ref[:half] = a_ref[...]
        all_ref[half:] = b_ref[...]
        rows = tree_rows(lambda k: all_ref[k], table, group_of(step)).astype(F32)
        out_ref[...] = dot(norm(rows, gain_ref[...]), w_ref[:, CWIDTH:]).astype(BF16)


def coarse_kernel(
    table, blocks, counts, pooled_ref, own_ref, left_ref, right_ref, far_a_ref, far_b_ref,
    gain_ref, w_ref, wo_ref, coarse_hbm, sent_ref, kv_ref, all_ref, att_ref, a_ref, b_ref, staged, sem,
):
    groups = lax.axis_size("grp")
    me = lax.axis_index("grp")
    rows = CWIDTH
    half = SUBS // 2
    all_ref[:half] = far_a_ref[...]
    all_ref[half:] = far_b_ref[...]
    far = norm(tree_rows(lambda k: all_ref[k], table, group_of(2)).astype(F32), gain_ref[...])
    at = pl.multiple_of(group_of(2) * rows, rows)
    kv_ref[pl.ds(at, rows)] = dot(far, w_ref[:, CWIDTH:]).astype(BF16)
    for step, ref in ((0, own_ref), (groups - 1, left_ref), (1, right_ref)):
        at = pl.multiple_of(group_of(step) * rows, rows)
        kv_ref[pl.ds(at, rows)] = ref[:, ref.shape[1] - 2 * CWIDTH :]
    size = 64
    lanes = lax.broadcasted_iota(jnp.int32, (1, 256), 1) // size
    keep = [(lanes == i).astype(F32) for i in range(4)]
    keep_low = [m.astype(BF16) for m in keep]
    member = lax.broadcasted_iota(jnp.int32, (1, MOST_BALL * CBLK), 1) // CBLK

    def members(b, at):
        starts = [pl.multiple_of(blocks[b * MOST_BALL + m] * CBLK, CBLK) for m in range(MOST_BALL)]
        return jnp.concatenate([kv_ref[pl.ds(s, CBLK), at : at + 256] for s in starts], axis=0)

    def score(dst, b, g):
        q = own_ref[pl.ds(pl.multiple_of(b * CBLK, CBLK), CBLK), 256 * g : 256 * g + 256]
        spread = jnp.concatenate([q * keep_low[i] for i in range(4)], axis=0)
        scores = dot(spread, members(b, 256 * g), NT) * (LOG2E / 8.0)
        dst[...] = jnp.where(member < counts[b], scores, -jnp.inf)

    def soft(src, b, g):
        scores = src[...]
        expo = jnp.exp2(scores - jnp.max(scores, axis=-1, keepdims=True))
        scale = 1.0 / jnp.sum(expo, axis=-1, keepdims=True)
        out = dot(expo.astype(BF16), members(b, CWIDTH + 256 * g)) * scale
        total = sum(out[CBLK * i : CBLK * (i + 1)] * keep[i] for i in range(4))
        begin = pl.multiple_of(b * CBLK, CBLK)
        att_ref[pl.ds(begin, CBLK), 256 * g : 256 * g + 256] = total.astype(BF16)

    count = rows // CBLK
    score(a_ref, 0, 0)

    def block(b, carry):
        score(b_ref, b, 1)
        soft(a_ref, b, 0)
        score(a_ref, jnp.minimum(b + 1, count - 1), 0)
        soft(b_ref, b, 1)
        return carry

    lax.fori_loop(0, count, block, 0, unroll=8)
    part = SUBS // 4
    for c in range(4):
        at = slice(part * POOL * c, part * POOL * (c + 1))
        result = pooled_ref[at].astype(F32) + dot(att_ref[at], wo_ref[...])
        result = result.astype(BF16).reshape(part, POOL, CWIDTH)
        staged[part * c : part * (c + 1)] = result
        near = pl.ds(part * c, part)
        pltpu.make_async_copy(staged.at[near], coarse_hbm.at[near], sem).start()
        for s in range(part):
            sent_ref[table[me, part * c + s]] = result[s]
    all_sent(staged, coarse_hbm, sem)


def call(kernel, outs, scratch, args, tables=1, flops=0, exps=0, name=None, grant=16, specs=None, out_specs=None):
    size = sum(a.size * a.dtype.itemsize for a in args)
    return pl.pallas_call(
        kernel,
        out_shape=outs,
        in_specs=specs or [SMEM] * tables + [VMEM] * (len(args) - tables),
        out_specs=out_specs if isinstance(out_specs, tuple) else jax.tree.map(lambda _: out_specs or VMEM, outs),
        scratch_shapes=scratch,
        name=name,
        compiler_params=pltpu.CompilerParams(vmem_limit_bytes=grant << 20),
        cost_estimate=pl.CostEstimate(flops=flops, bytes_accessed=2 * size, transcendentals=exps),
    )(*args)


def shaped(*shape):
    return jax.ShapeDtypeStruct(shape, BF16)


def exchange(pieces):
    return lax.all_to_all(pieces, "pts", split_axis=0, concat_axis=0, tiled=True)


def tables_of(rot_dest):
    points, groups = lax.axis_size("pts"), lax.axis_size("grp")
    point, group = lax.axis_index("pts"), lax.axis_index("grp")
    device = point * groups + group
    local = lax.dynamic_slice_in_dim(rot_dest, point * groups * SUBS, groups * SUBS)
    targets = (local // SUBS // groups).reshape(groups, SUBS)
    mine = lax.dynamic_index_in_dim(rot_dest.reshape(points, groups, SUBS), group, 1, False)
    slot = mine - device * SUBS
    source = jnp.arange(points, dtype=jnp.int32)
    hit = slot[None] == jnp.arange(SUBS, dtype=jnp.int32)[:, None, None]
    place = jnp.sum(jnp.where(hit, source[None, :, None], 0), axis=(1, 2))
    return targets, place.astype(jnp.int32)


def ball_table(order, sizes, count):
    total = order.shape[0]
    before = jnp.arange(sizes.shape[0])
    ends = jnp.sum(jnp.where(before[None, :] <= before[:, None], sizes[None, :], 0), axis=1)
    starts = ends - sizes
    marks = jnp.arange(total, dtype=jnp.int32)
    mine = lax.axis_index("grp") * count + jnp.arange(count, dtype=jnp.int32)
    where = jnp.sum(jnp.where(order[None, :] == mine[:, None], marks[None, :], 0), axis=1)
    inside = (starts[None, :] <= where[:, None]) & (where[:, None] < ends[None, :])
    first = jnp.sum(jnp.where(inside, starts[None, :], 0), axis=1)
    length = jnp.sum(jnp.where(inside, sizes[None, :], 0), axis=1)
    slots = jnp.arange(MOST_BALL, dtype=jnp.int32)
    place = jnp.minimum(first[:, None] + slots[None, :], total - 1)
    members = jnp.sum(
        jnp.where(place[:, :, None] == marks[None, None, :], order[None, None, :], 0), axis=2
    )
    return members.reshape(-1).astype(jnp.int32), length.astype(jnp.int32)


def body(
    points,
    rot_dest,
    block_order,
    ball_sizes,
    fine_gain,
    fine_qkv,
    fine_out,
    pool_weight,
    coarse_gain,
    coarse_qkv,
    coarse_out,
    unpool_weight,
):
    rows, width = points.shape
    groups = lax.axis_size("grp")
    crows = rows // 4
    wide = VM((2, BALL, 128), F32)
    cost = dict(flops=5 * 10**9, exps=4 * 10**6)
    sent = call(
        first_kernel,
        shaped(SUBS, SUB, width),
        [
            pltpu.SMEM(rot_dest.shape, jnp.int32),
            VM(fine_gain.shape, F32),
            VM((2 * width, width), BF16),
            VM((SUBS, SUB, width), BF16),
            VM((width, 3 * width), BF16),
            VM((width, width), BF16),
            VM((SUBS, SUB, width), BF16),
            pltpu.SemaphoreType.DMA((7,)),
        ]
        + FINE_SCRATCH,
        (rot_dest, fine_gain, points.reshape(SUBS, SUB, width), fine_qkv, fine_out),
        specs=[HBM] * 5,
        out_specs=HBM,
        name="first_layer",
        grant=60,
        **cost,
    )
    sent, rot_dest, block_order, ball_sizes, fine_qkv, fine_out, fine_gain = lax.optimization_barrier(
        (sent, rot_dest, block_order, ball_sizes, fine_qkv, fine_out, fine_gain)
    )
    targets, place = tables_of(rot_dest)
    members, lengths = ball_table(block_order[0], ball_sizes[0], crows // CBLK)
    packed = [fine_qkv[1], fine_qkv[2]]
    outer = [fine_out[1], fine_out[2]]

    arrived = exchange(sent)
    arrived, targets, place, members, lengths, packed, outer = lax.optimization_barrier(
        (arrived, targets, place, members, lengths, packed, outer)
    )
    second, pieces = call(
        second_kernel,
        (shaped(BALLS, BALL, width), shaped(SUBS, POOL, CWIDTH)),
        [VM((2 * width, width), BF16), wide, VM((BALLS, BALL // 4, 4 * width), BF16)] + FINE_SCRATCH,
        (place, arrived, fine_gain, packed[0], outer[0], pool_weight),
        name="second_layer",
        **cost,
    )
    pieces = exchange(pieces)
    up = [(i, (i + 1) % groups) for i in range(groups)]
    down = [(i, (i - 1) % groups) for i in range(groups)]
    half = SUBS // 2
    left_a = lax.ppermute(pieces[:half], "grp", up)
    right_b = lax.ppermute(pieces[half:], "grp", down)
    left_b = lax.ppermute(pieces[half:], "grp", up)
    right_a = lax.ppermute(pieces[:half], "grp", down)
    gain = coarse_gain[None]
    pooled, own = call(
        own_kernel,
        (shaped(crows, CWIDTH), shaped(crows, 3 * CWIDTH)),
        [],
        (targets, pieces, gain, coarse_qkv),
        flops=2 * crows * CWIDTH * 3 * CWIDTH,
        name="own_projection",
    )
    far_a = lax.ppermute(left_a, "grp", up)
    far_b = lax.ppermute(right_b, "grp", down)
    left, right = call(
        near_kernel,
        (shaped(crows, 2 * CWIDTH), shaped(crows, 2 * CWIDTH)),
        [VM((SUBS, POOL, CWIDTH), BF16)],
        (targets, left_a, left_b, right_a, right_b, gain, coarse_qkv),
        flops=8 * crows * CWIDTH * CWIDTH,
        name="near_projection",
    )
    coarse, pieces = call(
        coarse_kernel,
        (shaped(SUBS, POOL, CWIDTH), shaped(SUBS, POOL, CWIDTH)),
        [
            VM((groups * crows, 2 * CWIDTH), BF16),
            VM((SUBS, POOL, CWIDTH), BF16),
            VM((crows, CWIDTH), BF16),
            VM((4 * CBLK, MOST_BALL * CBLK), F32),
            VM((4 * CBLK, MOST_BALL * CBLK), F32),
            VM((SUBS, POOL, CWIDTH), BF16),
            pltpu.SemaphoreType.DMA,
        ],
        (targets, members, lengths, pooled, own, left, right, far_a, far_b, gain, coarse_qkv, coarse_out),
        tables=3,
        flops=4 * 10**9,
        exps=2 * 10**6,
        name="coarse_layer",
        out_specs=(HBM, VMEM),
        grant=24,
    )
    pieces = exchange(pieces)
    sent = call(
        third_kernel,
        shaped(SUBS, SUB, width),
        [
            VM((2 * width, width), BF16),
            wide,
            VM((BALLS, BALL // 4, 4 * width), F32),
            VM((BALLS, BALL, width), BF16),
        ]
        + FINE_SCRATCH,
        (place, second, pieces, fine_gain, packed[1], outer[1], unpool_weight),
        name="third_layer",
        **cost,
    )
    refined = call(
        ordered_kernel,
        shaped(SUBS, SUB, width),
        [pltpu.SemaphoreType.DMA],
        (targets, exchange(sent)),
        out_specs=HBM,
        name="ordered",
    )
    return refined.reshape(rows, width), coarse.reshape(crows, CWIDTH)


def solution(mesh):
    return jax.shard_map(
        body,
        mesh=mesh,
        in_specs=(
            P(("pts", "grp"), None),
            P(),
            P("pts", None),
            P("pts", None),
            P(),
            P(),
            P(),
            P(),
            P(),
            P(),
            P(),
            P(),
        ),
        out_specs=(P(("pts", "grp"), None), P(("pts", "grp"), None)),
        check_vma=False,
    )
```

```python
import functools
import math

import jax
import jax.numpy as jnp
from jax import lax
from jax.experimental import pallas as pl
from jax.experimental.pallas import tpu as pltpu
from jax.sharding import PartitionSpec as P

F32, BF16 = jnp.float32, jnp.bfloat16
HEADS = 8
BALL = 256
SUB = 64
CBLK = 64
MOST_BALL = 8
WIDTH = 256
CWIDTH = 512
SUBS = 32
POOL = 16
LOG2E = 1.4426950408889634
NT = (((1,), (1,)), ((), ()))
TN = (((0,), (0,)), ((), ()))
VMEM = pl.BlockSpec(memory_space=pltpu.VMEM)
SMEM = pl.BlockSpec(memory_space=pltpu.SMEM)


def dot(a, b, dims=None):
    if dims is None:
        return jnp.dot(a, b, preferred_element_type=F32)
    return lax.dot_general(a, b, dims, preferred_element_type=F32)


def norm(x, gain):
    return (x * lax.rsqrt(jnp.mean(x * x, axis=-1, keepdims=True) + 1e-6) * gain).astype(BF16)


SCALE = LOG2E / math.sqrt(32.0)
BALLS = SUBS // 4
VM = pltpu.VMEM
HBM = pl.BlockSpec(memory_space=pltpu.HBM)


def transposed(wqkv_ref, wqvt_ref):
    wqvt_ref[:WIDTH] = wqkv_ref[:, :WIDTH].T
    wqvt_ref[WIDTH:] = wqkv_ref[:, 2 * WIDTH :].T


def fine_layer(load, reload, store, send, gain, wqvt_ref, wk_ref, wo_ref, scores, bufs, ready=None):
    left, right = scores
    k_s, qt_s, vt_s, ot_s = bufs[0:2], bufs[2:4], bufs[4:6], bufs[6:8]
    ones = jnp.ones((16, BALL), BF16)

    def project(b, par):
        h = norm(load(b), gain)
        qv = dot(wqvt_ref[...], h, NT)
        qt_s[par][...] = (qv[:WIDTH] * SCALE).astype(BF16)
        vt_s[par][...] = qv[WIDTH:].astype(BF16)
        k_s[par][...] = dot(h, wk_ref[...]).astype(BF16)

    def score(dst, par, g, i):
        at = 32 * (4 * g + i)
        parts = [jnp.zeros((32 * i, BALL), BF16), qt_s[par][at : at + 32], jnp.zeros((96 - 32 * i, BALL), BF16)]
        query = jnp.concatenate([p for p in parts if p.shape[0]], axis=0)
        dst[BALL * i : BALL * (i + 1)] = dot(k_s[par][:, 128 * g : 128 * g + 128], query)

    def soft(src, par, g, i):
        s = src[BALL * i : BALL * (i + 1)]
        p = jnp.exp2(s - jnp.max(s, axis=0, keepdims=True)).astype(BF16)
        at = 32 * (4 * g + i)
        o = dot(jnp.concatenate([vt_s[par][at : at + 32], ones], axis=0), p)
        ot_s[par][at : at + 32] = (o[:32] * (1.0 / o[32:33])).astype(BF16)

    def finish(b, par):
        store(b, (reload(b) + dot(ot_s[par][...], wo_ref[...], TN)).astype(BF16))

    project(0, 0)
    for i in range(4):
        score(left, 0, 0, i)
    if ready is not None:
        ready()
    for b in range(BALLS):
        par, last = b % 2, b == BALLS - 1
        if send is not None and b % 2 == 0:
            for done in (b - 3, b - 2):
                if done >= 0:
                    send(done)
        if not last:
            project(b + 1, 1 - par)
        for i in range(4):
            score(right, par, 1, i)
            soft(left, par, 0, i)
        if b > 0:
            finish(b - 1, 1 - par)
        for i in range(4):
            if not last:
                score(left, 1 - par, 0, i)
            soft(right, par, 1, i)
    if send is not None:
        send(BALLS - 3)
        send(BALLS - 2)
    finish(BALLS - 1, (BALLS - 1) % 2)
    if send is not None:
        send(BALLS - 1)


def sent_to(staged, out, sem, at, to):
    pltpu.make_async_copy(staged.at[at], out.at[to], sem).start()


def all_sent(staged, out, sem):
    pltpu.make_async_copy(staged, out, sem).wait()


FINE_SCRATCH = [VM((4 * BALL, BALL), F32)] * 2 + [VM((BALL, WIDTH), BF16)] * 8


def first_kernel(
    rot_hbm, gain_hbm, x_hbm, wqkv_hbm, wo_hbm, out_hbm,
    rot, gain_ref, wqvt_ref, x_ref, wqkv_ref, wo_ref, staged, sems, *scratch
):
    groups = lax.axis_size("grp")
    device = lax.axis_index("pts") * groups + lax.axis_index("grp")
    query, key, value = [
        pltpu.make_async_copy(
            wqkv_hbm.at[0, :, pl.ds(WIDTH * c, WIDTH)], wqkv_ref.at[:, pl.ds(WIDTH * c, WIDTH)], sems.at[7 + c]
        )
        for c in range(3)
    ]
    early = pltpu.make_async_copy(x_hbm.at[pl.ds(0, 4)], x_ref.at[pl.ds(0, 4)], sems.at[1])
    gains = pltpu.make_async_copy(gain_hbm, gain_ref, sems.at[2])
    late = [
        pltpu.make_async_copy(x_hbm.at[pl.ds(4, SUBS - 4)], x_ref.at[pl.ds(4, SUBS - 4)], sems.at[3]),
        pltpu.make_async_copy(wo_hbm.at[0], wo_ref, sems.at[4]),
        pltpu.make_async_copy(rot_hbm, rot, sems.at[5]),
    ]
    for copy in (query, value, early, gains, key):
        copy.start()
    query.wait()
    wqvt_ref[:WIDTH] = wqkv_ref[:, :WIDTH].T
    value.wait()
    for copy in late:
        copy.start()
    wqvt_ref[WIDTH:] = wqkv_ref[:, 2 * WIDTH :].T
    early.wait()
    gains.wait()
    key.wait()

    def ready():
        for copy in late:
            copy.wait()

    def load(b):
        return x_ref[pl.ds(4 * b, 4)].reshape(BALL, WIDTH).astype(F32)

    def store(b, y):
        staged[pl.ds(4 * b, 4)] = y.reshape(4, SUB, WIDTH)

    def send(b):
        for i in range(4):
            to = rot[device * SUBS + 4 * b + i] // (SUBS * groups)
            sent_to(staged, out_hbm, sems.at[6], 4 * b + i, to)

    wk_ref = wqkv_ref.at[:, WIDTH : 2 * WIDTH]
    fine_layer(
        load, load, store, send, gain_ref[0:1], wqvt_ref, wk_ref, wo_ref, scratch[:2], scratch[2:], ready
    )
    all_sent(staged, out_hbm, sems.at[6])


def second_kernel(
    place, x_ref, gain_ref, wqkv_ref, wo_ref, pool_ref, out_ref, pooled_ref, wqvt_ref, wide_ref, rows_ref, *scratch
):
    transposed(wqkv_ref, wqvt_ref)
    wk_ref = wqkv_ref.at[:, WIDTH : 2 * WIDTH]

    def load(b):
        return jnp.concatenate([x_ref[place[4 * b + i]] for i in range(4)], axis=0).astype(F32)

    def store(b, y):
        out_ref[b] = y
        wide = y.astype(F32)
        for c in range(2):
            wide_ref[c] = wide[:, 128 * c : 128 * c + 128]
        rows_ref[b] = jnp.concatenate(
            [wide_ref[c, pl.ds(j, BALL // 4, stride=4)] for j in range(4) for c in range(2)],
            axis=1,
        ).astype(BF16)

    fine_layer(
        load, load, store, None, gain_ref[1:2], wqvt_ref, wk_ref, wo_ref, scratch[:2], scratch[2:]
    )
    part = BALLS // 2
    for b in range(0, BALLS, part):
        rows = rows_ref[b : b + part].reshape(part * BALL // 4, 4 * WIDTH)
        pooled = dot(rows, pool_ref[...]).astype(BF16)
        for i in range(4 * part):
            pooled_ref[place[4 * b + i]] = pooled[POOL * i : POOL * (i + 1)]


def third_kernel(
    place, x_ref, coarse_ref, gain_ref, wqkv_ref, wo_ref, unpool_ref, out_ref,
    wqvt_ref, wide_ref, lifted_ref, held_ref, *scratch
):
    transposed(wqkv_ref, wqvt_ref)
    wk_ref = wqkv_ref.at[:, WIDTH : 2 * WIDTH]

    part = BALLS // 2
    for b in range(0, BALLS, part):
        coarse = jnp.concatenate([coarse_ref[place[4 * b + i]] for i in range(4 * part)], axis=0)
        lifted_ref[b : b + part] = dot(coarse, unpool_ref[...]).reshape(part, BALL // 4, 4 * WIDTH)

    def load(b):
        for j in range(4):
            for c in range(2):
                at = WIDTH * j + 128 * c
                wide_ref[c, pl.ds(j, BALL // 4, stride=4)] = lifted_ref[b, :, at : at + 128]
        x = x_ref[b].astype(F32) + jnp.concatenate([wide_ref[0], wide_ref[1]], axis=1)
        held_ref[b] = x.astype(BF16)
        return x.astype(BF16).astype(F32)

    def reload(b):
        return held_ref[b].astype(F32)

    def store(b, y):
        for i in range(4):
            out_ref[place[4 * b + i]] = y[SUB * i : SUB * (i + 1)]

    fine_layer(
        load, reload, store, None, gain_ref[2:3], wqvt_ref, wk_ref, wo_ref, scratch[:2], scratch[2:]
    )


def ordered_kernel(table, x_ref, out_hbm, sem):
    me = lax.axis_index("grp")
    for s in range(SUBS):
        sent_to(x_ref, out_hbm, sem, table[me, s], s)
    all_sent(x_ref, out_hbm, sem)


def group_of(step):
    return lax.rem(lax.axis_index("grp") + step, lax.axis_size("grp"))


def tree_rows(pieces, table, group):
    return jnp.concatenate([pieces(table[group, s]) for s in range(SUBS)], axis=0)


def own_kernel(table, pieces_ref, gain_ref, w_ref, pooled_ref, out_ref):
    pooled_ref[...] = tree_rows(lambda k: pieces_ref[k], table, group_of(0))
    out_ref[...] = dot(norm(pooled_ref[...].astype(F32), gain_ref[...]), w_ref[...]).astype(BF16)


def near_kernel(table, la_ref, lb_ref, ra_ref, rb_ref, gain_ref, w_ref, left_ref, right_ref, all_ref):
    groups = lax.axis_size("grp")
    half = SUBS // 2
    for step, a_ref, b_ref, out_ref in ((groups - 1, la_ref, lb_ref, left_ref), (1, ra_ref, rb_ref, right_ref)):
        all_ref[:half] = a_ref[...]
        all_ref[half:] = b_ref[...]
        rows = tree_rows(lambda k: all_ref[k], table, group_of(step)).astype(F32)
        out_ref[...] = dot(norm(rows, gain_ref[...]), w_ref[:, CWIDTH:]).astype(BF16)


def coarse_kernel(
    table, blocks, counts, pooled_ref, own_ref, left_ref, right_ref, far_a_ref, far_b_ref,
    gain_ref, w_ref, wo_ref, coarse_hbm, sent_ref, kv_ref, all_ref, att_ref, a_ref, b_ref, staged, sem,
):
    groups = lax.axis_size("grp")
    me = lax.axis_index("grp")
    rows = CWIDTH
    half = SUBS // 2
    all_ref[:half] = far_a_ref[...]
    all_ref[half:] = far_b_ref[...]
    far = norm(tree_rows(lambda k: all_ref[k], table, group_of(2)).astype(F32), gain_ref[...])
    at = pl.multiple_of(group_of(2) * rows, rows)
    kv_ref[pl.ds(at, rows)] = dot(far, w_ref[:, CWIDTH:]).astype(BF16)
    for step, ref in ((0, own_ref), (groups - 1, left_ref), (1, right_ref)):
        at = pl.multiple_of(group_of(step) * rows, rows)
        kv_ref[pl.ds(at, rows)] = ref[:, ref.shape[1] - 2 * CWIDTH :]
    size = 64
    lanes = lax.broadcasted_iota(jnp.int32, (1, 256), 1) // size
    keep = [(lanes == i).astype(F32) for i in range(4)]
    keep_low = [m.astype(BF16) for m in keep]
    member = lax.broadcasted_iota(jnp.int32, (1, MOST_BALL * CBLK), 1) // CBLK

    def members(b, at):
        starts = [pl.multiple_of(blocks[b * MOST_BALL + m] * CBLK, CBLK) for m in range(MOST_BALL)]
        return jnp.concatenate([kv_ref[pl.ds(s, CBLK), at : at + 256] for s in starts], axis=0)

    def score(dst, b, g):
        q = own_ref[pl.ds(pl.multiple_of(b * CBLK, CBLK), CBLK), 256 * g : 256 * g + 256]
        spread = jnp.concatenate([q * keep_low[i] for i in range(4)], axis=0)
        scores = dot(spread, members(b, 256 * g), NT) * (LOG2E / 8.0)
        dst[...] = jnp.where(member < counts[b], scores, -jnp.inf)

    def soft(src, b, g):
        scores = src[...]
        expo = jnp.exp2(scores - jnp.max(scores, axis=-1, keepdims=True))
        scale = 1.0 / jnp.sum(expo, axis=-1, keepdims=True)
        out = dot(expo.astype(BF16), members(b, CWIDTH + 256 * g)) * scale
        total = sum(out[CBLK * i : CBLK * (i + 1)] * keep[i] for i in range(4))
        begin = pl.multiple_of(b * CBLK, CBLK)
        att_ref[pl.ds(begin, CBLK), 256 * g : 256 * g + 256] = total.astype(BF16)

    count = rows // CBLK
    score(a_ref, 0, 0)

    def block(b, carry):
        score(b_ref, b, 1)
        soft(a_ref, b, 0)
        score(a_ref, jnp.minimum(b + 1, count - 1), 0)
        soft(b_ref, b, 1)
        return carry

    lax.fori_loop(0, count, block, 0, unroll=8)
    part = SUBS // 4
    for c in range(4):
        at = slice(part * POOL * c, part * POOL * (c + 1))
        result = pooled_ref[at].astype(F32) + dot(att_ref[at], wo_ref[...])
        result = result.astype(BF16).reshape(part, POOL, CWIDTH)
        staged[part * c : part * (c + 1)] = result
        near = pl.ds(part * c, part)
        pltpu.make_async_copy(staged.at[near], coarse_hbm.at[near], sem).start()
        for s in range(part):
            sent_ref[table[me, part * c + s]] = result[s]
    all_sent(staged, coarse_hbm, sem)


def call(kernel, outs, scratch, args, tables=1, flops=0, exps=0, name=None, grant=16, specs=None, out_specs=None):
    size = sum(a.size * a.dtype.itemsize for a in args)
    return pl.pallas_call(
        kernel,
        out_shape=outs,
        in_specs=specs or [SMEM] * tables + [VMEM] * (len(args) - tables),
        out_specs=out_specs if isinstance(out_specs, tuple) else jax.tree.map(lambda _: out_specs or VMEM, outs),
        scratch_shapes=scratch,
        name=name,
        compiler_params=pltpu.CompilerParams(vmem_limit_bytes=grant << 20),
        cost_estimate=pl.CostEstimate(flops=flops, bytes_accessed=2 * size, transcendentals=exps),
    )(*args)


def shaped(*shape):
    return jax.ShapeDtypeStruct(shape, BF16)


def exchange(pieces):
    return lax.all_to_all(pieces, "pts", split_axis=0, concat_axis=0, tiled=True)


def tables_of(rot_dest):
    points, groups = lax.axis_size("pts"), lax.axis_size("grp")
    point, group = lax.axis_index("pts"), lax.axis_index("grp")
    device = point * groups + group
    local = lax.dynamic_slice_in_dim(rot_dest, point * groups * SUBS, groups * SUBS)
    targets = (local // SUBS // groups).reshape(groups, SUBS)
    mine = lax.dynamic_index_in_dim(rot_dest.reshape(points, groups, SUBS), group, 1, False)
    slot = mine - device * SUBS
    source = jnp.arange(points, dtype=jnp.int32)
    hit = slot[None] == jnp.arange(SUBS, dtype=jnp.int32)[:, None, None]
    place = jnp.sum(jnp.where(hit, source[None, :, None], 0), axis=(1, 2))
    return targets, place.astype(jnp.int32)


def ball_table(order, sizes, count):
    total = order.shape[0]
    before = jnp.arange(sizes.shape[0])
    ends = jnp.sum(jnp.where(before[None, :] <= before[:, None], sizes[None, :], 0), axis=1)
    starts = ends - sizes
    marks = jnp.arange(total, dtype=jnp.int32)
    mine = lax.axis_index("grp") * count + jnp.arange(count, dtype=jnp.int32)
    where = jnp.sum(jnp.where(order[None, :] == mine[:, None], marks[None, :], 0), axis=1)
    inside = (starts[None, :] <= where[:, None]) & (where[:, None] < ends[None, :])
    first = jnp.sum(jnp.where(inside, starts[None, :], 0), axis=1)
    length = jnp.sum(jnp.where(inside, sizes[None, :], 0), axis=1)
    slots = jnp.arange(MOST_BALL, dtype=jnp.int32)
    place = jnp.minimum(first[:, None] + slots[None, :], total - 1)
    members = jnp.sum(
        jnp.where(place[:, :, None] == marks[None, None, :], order[None, None, :], 0), axis=2
    )
    return members.reshape(-1).astype(jnp.int32), length.astype(jnp.int32)


def body(
    points,
    rot_dest,
    block_order,
    ball_sizes,
    fine_gain,
    fine_qkv,
    fine_out,
    pool_weight,
    coarse_gain,
    coarse_qkv,
    coarse_out,
    unpool_weight,
):
    rows, width = points.shape
    groups = lax.axis_size("grp")
    crows = rows // 4
    wide = VM((2, BALL, 128), F32)
    cost = dict(flops=5 * 10**9, exps=4 * 10**6)
    sent = call(
        first_kernel,
        shaped(SUBS, SUB, width),
        [
            pltpu.SMEM(rot_dest.shape, jnp.int32),
            VM(fine_gain.shape, F32),
            VM((2 * width, width), BF16),
            VM((SUBS, SUB, width), BF16),
            VM((width, 3 * width), BF16),
            VM((width, width), BF16),
            VM((SUBS, SUB, width), BF16),
            pltpu.SemaphoreType.DMA((10,)),
        ]
        + FINE_SCRATCH,
        (rot_dest, fine_gain, points.reshape(SUBS, SUB, width), fine_qkv, fine_out),
        specs=[HBM] * 5,
        out_specs=HBM,
        name="first_layer",
        grant=60,
        **cost,
    )
    sent, rot_dest, block_order, ball_sizes, fine_qkv, fine_out, fine_gain = lax.optimization_barrier(
        (sent, rot_dest, block_order, ball_sizes, fine_qkv, fine_out, fine_gain)
    )
    targets, place = tables_of(rot_dest)
    members, lengths = ball_table(block_order[0], ball_sizes[0], crows // CBLK)
    packed = [fine_qkv[1], fine_qkv[2]]
    outer = [fine_out[1], fine_out[2]]

    arrived = exchange(sent)
    arrived, targets, place, members, lengths, packed, outer = lax.optimization_barrier(
        (arrived, targets, place, members, lengths, packed, outer)
    )
    second, pieces = call(
        second_kernel,
        (shaped(BALLS, BALL, width), shaped(SUBS, POOL, CWIDTH)),
        [VM((2 * width, width), BF16), wide, VM((BALLS, BALL // 4, 4 * width), BF16)] + FINE_SCRATCH,
        (place, arrived, fine_gain, packed[0], outer[0], pool_weight),
        name="second_layer",
        **cost,
    )
    pieces = exchange(pieces)
    up = [(i, (i + 1) % groups) for i in range(groups)]
    down = [(i, (i - 1) % groups) for i in range(groups)]
    half = SUBS // 2
    left_a = lax.ppermute(pieces[:half], "grp", up)
    right_b = lax.ppermute(pieces[half:], "grp", down)
    left_b = lax.ppermute(pieces[half:], "grp", up)
    right_a = lax.ppermute(pieces[:half], "grp", down)
    gain = coarse_gain[None]
    pooled, own = call(
        own_kernel,
        (shaped(crows, CWIDTH), shaped(crows, 3 * CWIDTH)),
        [],
        (targets, pieces, gain, coarse_qkv),
        flops=2 * crows * CWIDTH * 3 * CWIDTH,
        name="own_projection",
    )
    far_a = lax.ppermute(left_a, "grp", up)
    far_b = lax.ppermute(right_b, "grp", down)
    left, right = call(
        near_kernel,
        (shaped(crows, 2 * CWIDTH), shaped(crows, 2 * CWIDTH)),
        [VM((SUBS, POOL, CWIDTH), BF16)],
        (targets, left_a, left_b, right_a, right_b, gain, coarse_qkv),
        flops=8 * crows * CWIDTH * CWIDTH,
        name="near_projection",
    )
    coarse, pieces = call(
        coarse_kernel,
        (shaped(SUBS, POOL, CWIDTH), shaped(SUBS, POOL, CWIDTH)),
        [
            VM((groups * crows, 2 * CWIDTH), BF16),
            VM((SUBS, POOL, CWIDTH), BF16),
            VM((crows, CWIDTH), BF16),
            VM((4 * CBLK, MOST_BALL * CBLK), F32),
            VM((4 * CBLK, MOST_BALL * CBLK), F32),
            VM((SUBS, POOL, CWIDTH), BF16),
            pltpu.SemaphoreType.DMA,
        ],
        (targets, members, lengths, pooled, own, left, right, far_a, far_b, gain, coarse_qkv, coarse_out),
        tables=3,
        flops=4 * 10**9,
        exps=2 * 10**6,
        name="coarse_layer",
        out_specs=(HBM, VMEM),
        grant=24,
    )
    pieces = exchange(pieces)
    sent = call(
        third_kernel,
        shaped(SUBS, SUB, width),
        [
            VM((2 * width, width), BF16),
            wide,
            VM((BALLS, BALL // 4, 4 * width), F32),
            VM((BALLS, BALL, width), BF16),
        ]
        + FINE_SCRATCH,
        (place, second, pieces, fine_gain, packed[1], outer[1], unpool_weight),
        name="third_layer",
        **cost,
    )
    refined = call(
        ordered_kernel,
        shaped(SUBS, SUB, width),
        [pltpu.SemaphoreType.DMA],
        (targets, exchange(sent)),
        out_specs=HBM,
        name="ordered",
    )
    return refined.reshape(rows, width), coarse.reshape(crows, CWIDTH)


def solution(mesh):
    return jax.shard_map(
        body,
        mesh=mesh,
        in_specs=(
            P(("pts", "grp"), None),
            P(),
            P("pts", None),
            P("pts", None),
            P(),
            P(),
            P(),
            P(),
            P(),
            P(),
            P(),
            P(),
        ),
        out_specs=(P(("pts", "grp"), None), P(("pts", "grp"), None)),
        check_vma=False,
    )
```
